256 devices in a mesh: gx: 32 (over y, z_lo, core), gy: 8 (over x, z_hi).
Axes of the slice: x: 4, y: 4, z: 8 (z_hi: 2, z_lo: 4; z = z_hi * 4 + z_lo), core: 2. Of those that a mesh axis runs over, the one named last changes fastest.
Arguments:
- solution_vector: float32 [3, 512, 128, 128], P(None, 'gx', 'gy'), may hold values from -1 to 3, as said below
- insulator_marker: int32 [512, 128, 128], P('gx', 'gy'), may hold values 0 or 1
- electrode_marker: int32 [512, 128, 128], P('gx', 'gy'), may hold values 0 or 1
- impurity_zone_index: int32 [128, 32, 32], P('gx', 'gy'), may hold values from 0 to 3
- conductivity_category: int32 [128, 32, 32], P('gx', 'gy'), may hold values from 0 to 3
- warmth_rise: float32 [128, 32, 32], P('gx', 'gy'), may hold values from 0 to 2
Outputs:
- new_state: float32 [3, 512, 128, 128], P(None, 'gx', 'gy')
- new_temperature: float32 [128, 32, 32], P('gx', 'gy')
The draws below stay inside these ranges and needn't reach their ends.
Inputs may be any that keep to these rules, and one draw needn't show every extreme that they name: `solution_vector`: channel 0 is the potential; channels 1 and 2 are the electron and hole densities, which are positive.
All inputs are finite; a program needn't handle non-finite values. No bound on the sum of `insulator_marker` or of `electrode_marker` on one device may be relied on, other than what follows from the above.
Results may differ from the reference program's by a relative error of at most 0.0003.
Values sent between devices are 32-bit elements; how exact they have to be, the bound alone decides.
A program may use at most 64 MiB of HBM per device.

```python
import math
import jax
import jax.numpy as jnp

LAYER_COUNT = 128
COARSEN_RATIO = 4
NEWTON = 3
SWEEPS = 3
COLUMN_COUNT = 512
ROW_COUNT = 128


def draw_solution_vector(key, part):
    key_pot = jax.random.fold_in(key, 11)
    species_label = jax.random.fold_in(key, 12)
    lattice_span = (COLUMN_COUNT, ROW_COUNT, LAYER_COUNT)
    voltage_field = jax.random.uniform(key_pot, lattice_span, jnp.float32, -0.5, 0.5)
    minimum_limit, maximum_limit = (0.5, 2.0)
    species_couple = jnp.exp(jax.random.uniform(species_label, (2,) + lattice_span, jnp.float32, math.log(minimum_limit), math.log(maximum_limit)))
    return jnp.concatenate([voltage_field[None], species_couple], 0)


def touch_ends(entries, key, smallest, largest):
    spot = [jax.random.randint(jax.random.fold_in(key, axis), (), 0, length) for axis, length in enumerate(entries.shape)]
    main_axis = entries.shape.index(max(entries.shape))
    neighbour = spot[:main_axis] + [(spot[main_axis] + 1) % entries.shape[main_axis]] + spot[main_axis + 1:]
    return entries.at[tuple(spot)].set(smallest).at[tuple(neighbour)].set(largest)


def block_scale(stream_key, extent, shards, smallest, largest):
    gain, own = 1.0, jax.random.fold_in(stream_key, 6)
    for axis_at, blocks in shards:
        heights = jnp.exp(jax.random.uniform(jax.random.fold_in(own, axis_at), (blocks,), jnp.float32, smallest / len(shards), largest / len(shards)))
        gain = gain * jnp.repeat(heights, extent[axis_at] // blocks).reshape([-1 if axis == axis_at else 1 for axis in range(len(extent))])
    return gain


def setup_inputs(seed: int = 0) -> dict:
    keys = jax.random.split(jax.random.key(seed), 7)
    solution_vector = draw_solution_vector(jax.random.fold_in(keys[6], 71), 0)
    insulator_marker = touch_ends((jax.random.randint(keys[1], (COLUMN_COUNT, ROW_COUNT, LAYER_COUNT), 0, 4) < 1).astype(jnp.int32), jax.random.fold_in(keys[1], 1), 0, 1)
    electrode_marker = touch_ends((jax.random.randint(keys[2], (COLUMN_COUNT, ROW_COUNT, LAYER_COUNT), 0, 16) < 1).astype(jnp.int32), jax.random.fold_in(keys[2], 1), 0, 1)
    impurity_zone_index = touch_ends(jax.random.randint(keys[3], (COLUMN_COUNT // COARSEN_RATIO, ROW_COUNT // COARSEN_RATIO, LAYER_COUNT // COARSEN_RATIO), 0, 4), jax.random.fold_in(keys[3], 1), 0, 3).astype(jnp.int32)
    conductivity_category = touch_ends(jax.random.randint(keys[4], (COLUMN_COUNT // COARSEN_RATIO, ROW_COUNT // COARSEN_RATIO, LAYER_COUNT // COARSEN_RATIO), 0, 4), jax.random.fold_in(keys[4], 1), 0, 3).astype(jnp.int32)
    warmth_rise = jnp.clip(2.0 * jax.random.uniform(keys[5], (COLUMN_COUNT // COARSEN_RATIO, ROW_COUNT // COARSEN_RATIO, LAYER_COUNT // COARSEN_RATIO), jnp.float32) ** block_scale(keys[5], (COLUMN_COUNT // COARSEN_RATIO, ROW_COUNT // COARSEN_RATIO, LAYER_COUNT // COARSEN_RATIO), ((0, 32), (1, 8)), -0.2, 0.2), 0.0, 2.0)
    return dict(solution_vector=solution_vector, insulator_marker=insulator_marker, electrode_marker=electrode_marker, impurity_zone_index=impurity_zone_index, conductivity_category=conductivity_category, warmth_rise=warmth_rise)


poisson_scale = 2.0
charge_scale = 4.0
clock_offset = 24.0
contact_bias = 0.25
heat_gain = 1.0
sink_rate = 0.3
speed_falloff = 0.5
dope_table = (-2.0, -0.5, 0.5, 2.0)
conduct_table = (0.5, 1.0, 2.0, 4.0)


def bernoulli(value):
    tiny = jnp.abs(value) < 1e-4
    safe = jnp.where(tiny, 1.0, jnp.expm1(value))
    return jnp.where(tiny, 1.0 - 0.5 * value, value / safe)


def bernoulli_slope(value):
    tiny = jnp.abs(value) < 0.05
    safe = jnp.where(tiny, 1.0, jnp.expm1(value))
    exact = (safe - value * jnp.exp(value)) / (safe * safe)
    series = -0.5 + value / 6.0 - value * value * value / 180.0
    return jnp.where(tiny, series, exact)


def neighbours(framed_array):
    return [framed_array[..., 2:, 1:-1, 1:-1], framed_array[..., :-2, 1:-1, 1:-1],
            framed_array[..., 1:-1, 2:, 1:-1], framed_array[..., 1:-1, :-2, 1:-1],
            framed_array[..., 1:-1, 1:-1, 2:], framed_array[..., 1:-1, 1:-1, :-2]]


def centre(framed_array):
    return framed_array[..., 1:-1, 1:-1, 1:-1]


def lookup(labels, table):
    result = jnp.zeros(labels.shape, jnp.float32)
    for level, amount in enumerate(table):
        result = result + jnp.where(labels == level, amount, 0.0)
    return result


def refine_warmth(coarse):
    lattice_span = coarse.shape
    spread = jnp.broadcast_to(coarse[:, None, :, None, :, None],
                              (lattice_span[0], COARSEN_RATIO, lattice_span[1], COARSEN_RATIO, lattice_span[2], COARSEN_RATIO))
    return spread.reshape(lattice_span[0] * COARSEN_RATIO, lattice_span[1] * COARSEN_RATIO, lattice_span[2] * COARSEN_RATIO)


def restrict(fine):
    lattice_span = fine.shape
    blocks = fine.reshape(lattice_span[0] // COARSEN_RATIO, COARSEN_RATIO, lattice_span[1] // COARSEN_RATIO, COARSEN_RATIO, lattice_span[2] // COARSEN_RATIO, COARSEN_RATIO)
    return jnp.mean(blocks, axis=(1, 3, 5))


def relax_weight(framed_array, warming_input, caloric_transfer):
    total = sum(neighbours(framed_array))
    return (warming_input + caloric_transfer * total) / (sink_rate + 6.0 * caloric_transfer)


def linearized_correction(framed_array, permittivity_framed, interior_frame_mask, impurity_profile, electrode_active, species_drift_speed):
    voltage_field = centre(framed_array[0])
    negative_density = centre(framed_array[1])
    positive_density = centre(framed_array[2])
    eps_here = centre(permittivity_framed)
    lap_sum = jnp.zeros_like(voltage_field)
    face_sum = jnp.zeros_like(voltage_field)
    negative_current = jnp.zeros_like(voltage_field)
    positive_current = jnp.zeros_like(voltage_field)
    negative_gradient = jnp.zeros_like(voltage_field)
    positive_gradient = jnp.zeros_like(voltage_field)
    backward_scharfetter = jnp.zeros_like(voltage_field)
    forward_scharfetter = jnp.zeros_like(voltage_field)
    ohmic_dissipation = jnp.zeros_like(voltage_field)
    parts = zip(neighbours(framed_array[0]), neighbours(framed_array[1]), neighbours(framed_array[2]),
                neighbours(permittivity_framed), neighbours(interior_frame_mask))
    for pot_near, elec_near, hole_near, eps_near, weight in parts:
        drop = pot_near - voltage_field
        plus = bernoulli(drop)
        minus = bernoulli(-drop)
        slope_plus = bernoulli_slope(drop)
        slope_minus = bernoulli_slope(-drop)
        face = weight * 0.5 * (eps_here + eps_near)
        lap_sum = lap_sum + face * drop
        face_sum = face_sum + face
        elec_flow = weight * (elec_near * plus - negative_density * minus)
        hole_flow = weight * (hole_near * minus - positive_density * plus)
        negative_current = negative_current + elec_flow
        positive_current = positive_current + hole_flow
        ohmic_dissipation = ohmic_dissipation + (elec_flow - hole_flow) * (elec_flow - hole_flow)
        negative_gradient = negative_gradient + weight * (-elec_near * slope_plus - negative_density * slope_minus)
        positive_gradient = positive_gradient + weight * (hole_near * slope_minus + positive_density * slope_plus)
        backward_scharfetter = backward_scharfetter + weight * minus
        forward_scharfetter = forward_scharfetter + weight * plus
    denom = negative_density + positive_density + 2.0
    annihilation_rate = (negative_density * positive_density - 1.0) / denom
    negative_generation = (positive_density + 1.0) * (positive_density + 1.0) / (denom * denom)
    positive_generation = (negative_density + 1.0) * (negative_density + 1.0) / (denom * denom)
    res_psi = poisson_scale * lap_sum + charge_scale * (positive_density - negative_density + impurity_profile)
    negative_mismatch = species_drift_speed * negative_current - annihilation_rate
    positive_mismatch = species_drift_speed * positive_current - annihilation_rate
    blank_array = jnp.zeros_like(voltage_field)
    unit_array = jnp.ones_like(voltage_field)
    res_psi = jnp.where(electrode_active, voltage_field - contact_bias * impurity_profile, res_psi)
    negative_mismatch = jnp.where(electrode_active, negative_density - 1.0, negative_mismatch)
    positive_mismatch = jnp.where(electrode_active, positive_density - 1.0, positive_mismatch)
    mat_aa = jnp.where(electrode_active, unit_array, -poisson_scale * face_sum)
    mat_ab = jnp.where(electrode_active, blank_array, -charge_scale * unit_array)
    mat_ac = jnp.where(electrode_active, blank_array, charge_scale * unit_array)
    jacobian_entry_second_first = jnp.where(electrode_active, blank_array, species_drift_speed * negative_gradient)
    jacobian_entry_second_second = jnp.where(electrode_active, unit_array, -species_drift_speed * backward_scharfetter - negative_generation - clock_offset)
    mat_bc = jnp.where(electrode_active, blank_array, -positive_generation)
    jacobian_entry_third_first = jnp.where(electrode_active, blank_array, species_drift_speed * positive_gradient)
    mat_cb = jnp.where(electrode_active, blank_array, -negative_generation)
    jacobian_entry_third_third = jnp.where(electrode_active, unit_array, -species_drift_speed * forward_scharfetter - positive_generation - clock_offset)
    cof_aa = jacobian_entry_second_second * jacobian_entry_third_third - mat_bc * mat_cb
    cof_ab = mat_bc * jacobian_entry_third_first - jacobian_entry_second_first * jacobian_entry_third_third
    cof_ac = jacobian_entry_second_first * mat_cb - jacobian_entry_second_second * jacobian_entry_third_first
    determ = mat_aa * cof_aa + mat_ab * cof_ab + mat_ac * cof_ac
    step_psi = (cof_aa * res_psi + (mat_ac * mat_cb - mat_ab * jacobian_entry_third_third) * negative_mismatch
                + (mat_ab * mat_bc - mat_ac * jacobian_entry_second_second) * positive_mismatch) / determ
    step_n = (cof_ab * res_psi + (mat_aa * jacobian_entry_third_third - mat_ac * jacobian_entry_third_first) * negative_mismatch
              + (mat_ac * jacobian_entry_second_first - mat_aa * mat_bc) * positive_mismatch) / determ
    step_p = (cof_ac * res_psi + (mat_ab * jacobian_entry_third_first - mat_aa * mat_cb) * negative_mismatch
              + (mat_aa * jacobian_entry_second_second - mat_ab * jacobian_entry_second_first) * positive_mismatch) / determ
    new_pot = voltage_field - step_psi
    new_elec = negative_density * jnp.exp(-step_n / negative_density)
    new_hole = positive_density * jnp.exp(-step_p / positive_density)
    warming_field = 0.5 * species_drift_speed * ohmic_dissipation / (negative_density + positive_density)
    return jnp.stack([new_pot, new_elec, new_hole], 0), warming_field


def reference(solution_vector, insulator_marker, electrode_marker, impurity_zone_index, conductivity_category, warmth_rise):
    eps = jnp.where(insulator_marker == 1, 0.4, 1.0).astype(solution_vector.dtype)
    permittivity_framed = jnp.pad(eps, 1)
    interior_frame_mask = jnp.pad(jnp.ones_like(eps), 1)
    impurity_profile = refine_warmth(lookup(impurity_zone_index, dope_table))
    caloric_transfer = lookup(conductivity_category, conduct_table)
    electrode_active = electrode_marker == 1
    for newton_step in range(NEWTON):
        species_drift_speed = 1.0 / (1.0 + speed_falloff * refine_warmth(warmth_rise))
        framed_array = jnp.pad(solution_vector, ((0, 0), (1, 1), (1, 1), (1, 1)))
        solution_vector, warming_field = linearized_correction(framed_array, permittivity_framed, interior_frame_mask, impurity_profile, electrode_active, species_drift_speed)
        warming_input = heat_gain * restrict(warming_field)
        for sweep in range(SWEEPS):
            warmth_rise = relax_weight(jnp.pad(warmth_rise, 1), warming_input, caloric_transfer)
    return solution_vector, warmth_rise
```

```python
import functools

import jax
import jax.numpy as jnp
from jax import lax
from jax.experimental import pallas as pl
from jax.experimental.pallas import tpu as pltpu
from jax.sharding import PartitionSpec as P

NEWTON = 3
SWEEPS = 3
SIDE = 16
LANES = 128
CELLS = 4
NODES = SIDE * SIDE

CHARGE = 4.0
SHIFT = 24.0
BIAS = 0.25
HEAT_GAIN = 1.0
SINK = 0.3
DROP = 0.5

F32 = jnp.float32
MESH = pl.DeviceIdType.MESH
OPPOSITE = (1, 0, 3, 2)
DIAGONAL_OPPOSITE = (3, 2, 1, 0)


def face(pi, ni, qi, pj, nj, qj):
    d = pj - pi
    u = jnp.abs(d)
    v = d * d
    small = u < 0.5
    r = 1.0 / (jnp.exp(u) - 1.0)
    wide = u * r
    g_near = 1.0 + v * (1.0 / 12.0 + v * (-1.0 / 720.0 + v * (1.0 / 30240.0 + v * (-1.0 / 1209600.0))))
    h_near = u * (1.0 / 6.0 + v * (-1.0 / 180.0 + v * (1.0 / 5040.0 + v * (-1.0 / 151200.0))))
    b = jnp.where(small, g_near - 0.5 * u, wide)
    h = jnp.where(small, h_near, r * (1.0 - wide) - wide + 0.5)
    g = b + 0.5 * u
    h = jnp.where(d < 0.0, -h, h)
    plus = b + jnp.maximum(-d, 0.0)
    minus = b + jnp.maximum(d, 0.0)
    je = nj * plus - ni * minus
    jh = qj * minus - qi * plus
    gn = 0.5 * (nj + ni) - h * (nj - ni)
    gp = -0.5 * (qj + qi) - h * (qj - qi)
    return d, je, jh, gn, gp, g


def spread(a, lane):
    a = a + jnp.where((lane & 1) == 0, pltpu.roll(a, LANES - 1, 1), pltpu.roll(a, 1, 1))
    return a + jnp.where((lane & 2) == 0, pltpu.roll(a, LANES - 2, 1), pltpu.roll(a, 2, 1))


def body(
    nx, ny,
    sol_ref, ins_ref, ele_ref, imp_ref, con_ref, war_ref,
    out_ref, temp_ref,
    st, eps, ins, ele, wl, fc, acc, hs, yq, mob, dop, rep, small, wbx, wby,
    hx, hy, hex_, se, sy, ts, ds, tr, dr, tx, sx, cx, ix, dd,
    load_sem, store_sem, s_send, s_recv, e_send, e_recv, t_send, t_recv, d_send, d_recv,
):
    gx = lax.axis_index("gx")
    gy = lax.axis_index("gy")
    xl, xh = lax.rem(gx + nx - 1, nx), lax.rem(gx + 1, nx)
    yl, yh = lax.rem(gy + ny - 1, ny), lax.rem(gy + 1, ny)
    near = ((xl, gy), (xh, gy), (gx, yl), (gx, yh))
    corner = ((xl, yl), (xl, yh), (xh, yl), (xh, yh))
    has = (gx > 0, gx < nx - 1, gy > 0, gy < ny - 1)
    has_corner = (has[0] & has[2], has[0] & has[3], has[1] & has[2], has[1] & has[3])

    barrier = pltpu.get_barrier_semaphore()
    for target in near + corner:
        pl.semaphore_signal(barrier, inc=1, device_id=target, device_id_type=MESH)

    loads = [
        pltpu.make_async_copy(sol_ref, st, load_sem.at[0]),
        pltpu.make_async_copy(ins_ref, ins, load_sem.at[1]),
        pltpu.make_async_copy(ele_ref, ele, load_sem.at[2]),
    ]
    for copy in loads:
        copy.start()

    lane = lax.broadcasted_iota(jnp.int32, (1, LANES), 1)
    lane4 = lane & 3
    last_lane = (lane != LANES - 1).astype(F32)
    last_row = (lax.broadcasted_iota(jnp.int32, (SIDE, LANES), 0) != SIDE - 1).astype(F32)

    def slab(x):
        return pl.ds(pl.multiple_of(x * SIDE, SIDE), SIDE)

    def remote(src, dst, send, recv, target):
        return pltpu.make_async_remote_copy(
            src_ref=src, dst_ref=dst, send_sem=send, recv_sem=recv, device_id=target, device_id_type=MESH
        )

    def state_copies(k):
        out = []
        for s in range(4):
            if s < 2:
                src = st.at[:, pl.ds(0 if s == 0 else NODES - SIDE, SIDE), :]
                dst = hx.at[k, OPPOSITE[s]]
            else:
                src, dst = sy.at[s - 2], hy.at[k, OPPOSITE[s] - 2]
            out.append(remote(src, dst, s_send.at[k, s], s_recv.at[k, OPPOSITE[s]], near[s]))
        return out

    def eps_copies():
        out = []
        for s in range(4):
            src = eps.at[pl.ds(0 if s == 0 else NODES - SIDE, SIDE), :] if s < 2 else se.at[s - 2]
            out.append(remote(src, hex_.at[OPPOSITE[s]], e_send.at[s], e_recv.at[OPPOSITE[s]], near[s]))
        return out

    def thermal_copies(t):
        out = []
        for s in range(4):
            o = OPPOSITE[s]
            out.append(remote(ts.at[t], tr.at[t, o], t_send.at[t, s], t_recv.at[t, o], near[s]))
        for s in range(4):
            o = DIAGONAL_OPPOSITE[s]
            out.append(remote(ds.at[t, s], dr.at[t, o], d_send.at[t, s], d_recv.at[t, o], corner[s]))
        return out

    def pack_rows():
        for f in range(3):
            sy[0, f] = st[f, pl.ds(0, SIDE, stride=SIDE), :]
            sy[1, f] = st[f, pl.ds(SIDE - 1, SIDE, stride=SIDE), :]

    def pack_thermal(t, warm, source):
        ts[t, 0:4, :] = warm
        ts[t, 4:8, :] = source
        tile = ts[t]
        up2, down2 = pltpu.roll(tile, 2, 1), pltpu.roll(tile, LANES - 2, 1)
        up3, down3 = pltpu.roll(tile, 3, 1), pltpu.roll(tile, LANES - 3, 1)

        def low(a, b):
            return jnp.where(lane4 < 2, tile[a:a + 1], jnp.where(lane4 == 2, up2[b:b + 1], up3[a + 4:a + 5]))

        def high(a, b):
            return jnp.where(lane4 >= 2, tile[a:a + 1], jnp.where(lane4 == 1, down2[b:b + 1], down3[a + 4:a + 5]))

        ds[t, 0] = low(0, 1)
        ds[t, 1] = high(0, 1)
        ds[t, 2] = low(3, 2)
        ds[t, 3] = high(3, 2)

    def keep(flag, a):
        return jnp.where(flag, a, jnp.zeros_like(a))

    def load_corners(t):
        for s in range(4):
            dd[s:s + 1, :] = keep(has_corner[s], dr[t, s])

    def gather_source(t, into):
        tile = dd[...]
        up3, down3 = pltpu.roll(tile, 3, 1), pltpu.roll(tile, LANES - 3, 1)
        into[1, 0:2, :] = keep(has[0], tr[t, 0, 6:8, :])
        into[1, 2:6, :] = ts[t, 4:8, :]
        into[1, 6:8, :] = keep(has[1], tr[t, 1, 4:6, :])
        into[0, 2:6, :] = keep(has[2], tr[t, 2, 4:8, :])
        into[2, 2:6, :] = keep(has[3], tr[t, 3, 4:8, :])
        into[0, 1:2, :] = up3[0:1]
        into[0, 6:7, :] = up3[2:3]
        into[2, 1:2, :] = down3[1:2]
        into[2, 6:7, :] = down3[3:4]

    def gather_warm(t):
        tile = dd[...]
        up2, down2 = pltpu.roll(tile, 2, 1), pltpu.roll(tile, LANES - 2, 1)
        tx[1, 0:3, :] = keep(has[0], tr[t, 0, 1:4, :])
        tx[1, 3:7, :] = ts[t, 0:4, :]
        tx[1, 7:10, :] = keep(has[1], tr[t, 1, 0:3, :])
        tx[0, 3:7, :] = keep(has[2], tr[t, 2, 0:4, :])
        tx[2, 3:7, :] = keep(has[3], tr[t, 3, 0:4, :])
        tx[0, 1:2, :] = up2[0:1]
        tx[0, 2:3, :] = tile[0:1]
        tx[0, 7:8, :] = tile[2:3]
        tx[0, 8:9, :] = up2[2:3]
        tx[2, 1:2, :] = down2[1:2]
        tx[2, 2:3, :] = tile[1:2]
        tx[2, 7:8, :] = tile[3:4]
        tx[2, 8:9, :] = down2[3:4]

    def relax(t):
        load_corners(t)
        gather_source(t, sx)
        gather_warm(t)
        for _ in range(SWEEPS):
            mid = [tx[b, 1:9, :] for b in range(3)]
            new = []
            for b in range(3):
                c = mid[b]
                z_low = jnp.where(lane >= 4, pltpu.roll(c, 4, 1), 0.0)
                z_high = jnp.where(lane < LANES - 4, pltpu.roll(c, LANES - 4, 1), 0.0)
                y_low, y_high = pltpu.roll(c, 1, 1), pltpu.roll(c, LANES - 1, 1)
                if b > 0:
                    y_low = jnp.where(lane4 > 0, y_low, pltpu.roll(mid[b - 1], LANES - 3, 1))
                if b < 2:
                    y_high = jnp.where(lane4 < 3, y_high, pltpu.roll(mid[b + 1], 3, 1))
                total = (tx[b, 0:8, :] + tx[b, 2:10, :]) + (y_low + y_high) + (z_low + z_high)
                new.append((sx[b] + cx[b] * total) * ix[b])
            for b in range(3):
                tx[b, 1:9, :] = new[b]
        return tx[1, 3:7, :]

    def lookup(labels, table):
        result = jnp.zeros(labels.shape, F32)
        for level, amount in enumerate(table):
            result = jnp.where(labels == level, amount, result)
        return result

    for c in range(CELLS):
        small[4 * c:4 * c + 4, :] = lookup(imp_ref[c], (-2.0, -0.5, 0.5, 2.0))
        small[16 + 4 * c:16 + 4 * c + 4, :] = lookup(con_ref[c], (0.5, 1.0, 2.0, 4.0))
        small[32 + 4 * c:32 + 4 * c + 4, :] = war_ref[c]
    zc = LANES // 4
    wide = (lax.broadcasted_iota(jnp.int32, (zc, LANES), 1) // 4 == lax.broadcasted_iota(jnp.int32, (zc, LANES), 0)).astype(F32)
    rep[...] = jnp.dot(small[...], wide, precision=lax.Precision.HIGHEST, preferred_element_type=F32)
    for c in range(CELLS):
        for y in range(CELLS):
            dop[c, 4 * y:4 * y + 4, :] = jnp.broadcast_to(rep[4 * c + y:4 * c + y + 1, :], (4, LANES))

    def packed(first):
        rows = [rep[pl.ds(first + y, 4, stride=4), :] for y in range(CELLS)]
        return jnp.where(lane4 == 0, rows[0], jnp.where(lane4 == 1, rows[1], jnp.where(lane4 == 2, rows[2], rows[3])))

    cond, warm0 = packed(16), packed(32)
    pack_thermal(0, cond, cond)
    ts[1, 0:4, :] = warm0
    tx[...] = jnp.zeros_like(tx)
    sx[...] = jnp.zeros_like(sx)
    cx[...] = jnp.zeros_like(cx)
    dd[...] = jnp.zeros_like(dd)

    for copy in loads:
        copy.wait()
    pack_rows()
    eps[...] = jnp.where(ins[...] == 1, 0.4, 1.0).astype(F32)
    se[0] = eps[pl.ds(0, SIDE, stride=SIDE), :]
    se[1] = eps[pl.ds(SIDE - 1, SIDE, stride=SIDE), :]

    pl.semaphore_wait(barrier, 8)
    for copy in state_copies(0) + eps_copies() + thermal_copies(0):
        copy.start()

    def weigh(x, below, upper):
        e = eps[slab(x), :]
        wy = (e + pltpu.roll(e, SIDE - 1, 0)) * last_row
        wz = (e + pltpu.roll(e, LANES - 1, 1)) * last_lane
        wl[1, slab(x), :] = wy
        wl[2, slab(x), :] = wz
        total = below + wy + pltpu.roll(wy, 1, 0) + wz + pltpu.roll(wz, 1, 1)
        if not upper:
            fc[slab(x), :] = total
            return below
        wx = e + eps[slab(x + 1), :]
        wl[0, slab(x), :] = wx
        fc[slab(x), :] = total + wx
        return wx

    zero = jnp.zeros((SIDE, LANES), F32)
    below = lax.fori_loop(0, SIDE - 1, lambda x, b: weigh(x, b, True), zero)
    weigh(SIDE - 1, below, False)

    def fluxes(x, below, upper):
        psi, n, p = (st[f, slab(x), :] for f in range(3))
        d, je, jh, gn, gp, g = face(psi, n, p, *(pltpu.roll(a, SIDE - 1, 0) for a in (psi, n, p)))
        je, jh, gn, gp, g, ld = (a * last_row for a in (je, jh, gn, gp, g, d))
        lap = wl[1, slab(x), :] * d
        t = je - jh
        sums = [je, jh, lap, ld, gn, gp, g, t * t]
        sums = [a - pltpu.roll(a, 1, 0) if i < 4 else a + pltpu.roll(a, 1, 0) for i, a in enumerate(sums)]
        d, je, jh, gn, gp, g = face(psi, n, p, *(pltpu.roll(a, LANES - 1, 1) for a in (psi, n, p)))
        je, jh, gn, gp, g, ld = (a * last_lane for a in (je, jh, gn, gp, g, d))
        lap = wl[2, slab(x), :] * d
        t = je - jh
        more = [je, jh, lap, ld, gn, gp, g, t * t]
        more = [a - pltpu.roll(a, 1, 1) if i < 4 else a + pltpu.roll(a, 1, 1) for i, a in enumerate(more)]
        sums = [a + b for a, b in zip(sums, more)]
        sums = [a - b if i < 4 else a + b for i, (a, b) in enumerate(zip(sums, below))]
        carry = below
        if upper:
            d, je, jh, gn, gp, g = face(psi, n, p, *(st[f, slab(x + 1), :] for f in range(3)))
            t = je - jh
            carry = (je, jh, wl[0, slab(x), :] * d, d, gn, gp, g, t * t)
            sums = [a + b for a, b in zip(sums, carry)]
        for q in range(7):
            acc[q, slab(x), :] = sums[q]
        cell = slab(x // CELLS)
        hs[cell, :] = hs[cell, :] + sums[7] / (n + p)
        return carry

    def edge(side, mine, halo, weight):
        scale = has[side].astype(F32)
        if side % 2 == 0:
            d, je, jh, gn, gp, g = face(*halo, *mine)
            sign = -scale
        else:
            d, je, jh, gn, gp, g = face(*mine, *halo)
            sign = scale
        t = (je - jh) * scale
        return (je * sign, jh * sign, weight * d * sign, d * sign, gn * scale, gp * scale, g * scale), t * t

    def step(k, nothing):
        hs[...] = jnp.zeros_like(hs)
        none = (zero,) * 8
        below = lax.fori_loop(0, SIDE - 1, lambda x, b: fluxes(x, b, True), none)
        fluxes(SIDE - 1, below, False)

        @pl.when(k == 0)
        def _():
            for copy in eps_copies() + thermal_copies(0):
                copy.wait()
            for s in range(2):
                rows = pl.ds(s * (NODES - SIDE), SIDE)
                wbx[s] = eps[rows, :] + hex_[s]
                fc[rows, :] = fc[rows, :] + wbx[s] * has[s].astype(F32)
            for s in range(2):
                rows = pl.ds(s * (SIDE - 1), SIDE, stride=SIDE)
                wby[s] = se[s] + hex_[2 + s]
                fc[rows, :] = fc[rows, :] + wby[s] * has[2 + s].astype(F32)
            load_corners(0)
            gather_source(0, cx)
            ix[...] = 1.0 / (SINK + 6.0 * cx[...])

        @pl.when(k > 0)
        def _():
            for copy in thermal_copies(k):
                copy.wait()
            ts[k + 1, 0:4, :] = relax(k)

        warm = ts[k + 1, 0:4, :]
        m = 1.0 / (1.0 + DROP * warm)
        m4 = spread(jnp.concatenate([jnp.where(lane4 == y, m, 0.0) for y in range(CELLS)], 0), lane)
        rep[0:16, :] = m4
        for c in range(CELLS):
            for y in range(CELLS):
                mob[c, 4 * y:4 * y + 4, :] = jnp.broadcast_to(rep[4 * y + c:4 * y + c + 1, :], (4, LANES))

        for copy in state_copies(k):
            copy.wait()
        for s in range(2):
            rows = pl.ds(s * (NODES - SIDE), SIDE)
            mine = [st[f, rows, :] for f in range(3)]
            sums, heat = edge(s, mine, [hx[k, s, f] for f in range(3)], wbx[s])
            for q in range(7):
                acc[q, rows, :] = acc[q, rows, :] + sums[q]
            cell = pl.ds(s * (64 - SIDE), SIDE)
            hs[cell, :] = hs[cell, :] + heat / (mine[1] + mine[2])
        for s in range(2):
            rows = pl.ds(s * (SIDE - 1), SIDE, stride=SIDE)
            mine = [sy[s, f] for f in range(3)]
            sums, heat = edge(2 + s, mine, [hy[k, s, f] for f in range(3)], wby[s])
            for q in range(7):
                acc[q, rows, :] = acc[q, rows, :] + sums[q]
            yq[s] = heat / (mine[1] + mine[2])

        parts = []
        for y in range(CELLS):
            total = hs[pl.ds(4 * y, 4, stride=SIDE), :]
            for i in range(1, 4):
                total = total + hs[pl.ds(4 * y + i, 4, stride=SIDE), :]
            if y in (0, CELLS - 1):
                for i in range(4):
                    total = total + yq[y // (CELLS - 1), pl.ds(i, 4, stride=4), :]
            parts.append(total)
        rep[0:16, :] = spread(jnp.concatenate(parts, 0), lane)
        r = [rep[4 * y:4 * y + 4, :] for y in range(CELLS)]
        heat = jnp.where(lane4 == 0, r[0], jnp.where(lane4 == 1, r[1], jnp.where(lane4 == 2, r[2], r[3])))
        pack_thermal(k + 1, warm, heat * m * (HEAT_GAIN * 0.5 / 64.0))
        for copy in thermal_copies(k + 1):
            copy.start()

        def solve(x, nothing):
            rows = slab(x)
            psi, n, p = (st[f, rows, :] for f in range(3))
            fe, fh, lap, ls, gn, gp, gs = (acc[q, rows, :] for q in range(7))
            cell = x // CELLS
            mu, level = mob[cell], dop[cell]
            contact = ele[rows, :] == 1
            rd = 1.0 / (n + p + 2.0)
            rec = (n * p - 1.0) * rd
            rn, rp = (p + 1.0) * rd, (n + 1.0) * rd
            rn, rp = rn * rn, rp * rp
            r0 = lap + CHARGE * (p - n + level)
            r1 = mu * fe - rec
            r2 = mu * fh - rec
            aa = -fc[rows, :]
            ba, ca = mu * gn, mu * gp
            bb = -mu * (gs + 0.5 * ls) - rn - SHIFT
            cc = -mu * (gs - 0.5 * ls) - rp - SHIFT
            bc, cb = -rp, -rn
            c_aa = bb * cc - bc * cb
            c_ab = bc * ca - ba * cc
            c_ac = ba * cb - bb * ca
            inv = 1.0 / (aa * c_aa + CHARGE * (c_ac - c_ab))
            d0 = (c_aa * r0 + CHARGE * ((cb + cc) * r1 - (bc + bb) * r2)) * inv
            d1 = (c_ab * r0 + (aa * cc - CHARGE * ca) * r1 + (CHARGE * ba - aa * bc) * r2) * inv
            d2 = (c_ac * r0 - (CHARGE * ca + aa * cb) * r1 + (aa * bb + CHARGE * ba) * r2) * inv
            d0 = jnp.where(contact, psi - BIAS * level, d0)
            d1 = jnp.where(contact, n - 1.0, d1)
            d2 = jnp.where(contact, p - 1.0, d2)
            st[0, rows, :] = psi - d0
            st[1, rows, :] = n * jnp.exp(-d1 / n)
            st[2, rows, :] = p * jnp.exp(-d2 / p)
            return nothing

        lax.fori_loop(0, SIDE, solve, 0)

        @pl.when(k < NEWTON - 1)
        def _():
            pack_rows()
            for copy in state_copies(k + 1):
                copy.start()

        return nothing

    lax.fori_loop(0, NEWTON, step, 0)

    store = pltpu.make_async_copy(st, out_ref, store_sem)
    store.start()
    for copy in thermal_copies(NEWTON):
        copy.wait()
    warm = relax(NEWTON)
    cells = jnp.concatenate([jnp.where(lane4 == y, warm, 0.0) for y in range(CELLS)], 0)
    narrow = (lax.broadcasted_iota(jnp.int32, (LANES, zc), 0) // 4 == lax.broadcasted_iota(jnp.int32, (LANES, zc), 1)).astype(F32)
    cells = jnp.dot(cells, narrow, precision=lax.Precision.HIGHEST, preferred_element_type=F32)
    for c in range(CELLS):
        for y in range(CELLS):
            temp_ref[c, y:y + 1, :] = cells[4 * y + c:4 * y + c + 1, :]
    store.wait()


def solution(mesh):
    nx, ny = mesh.shape["gx"], mesh.shape["gy"]

    def per_device(sol, ins, ele, imp, con, war):
        vm = pltpu.VMEM
        dma = pltpu.SemaphoreType.DMA
        tile = (SIDE, LANES)
        call = pl.pallas_call(
            functools.partial(body, nx, ny),
            out_shape=(
                jax.ShapeDtypeStruct((3, NODES, LANES), F32),
                jax.ShapeDtypeStruct((CELLS, CELLS, LANES // 4), F32),
            ),
            in_specs=[pl.BlockSpec(memory_space=pl.ANY)] * 3 + [pl.BlockSpec(memory_space=pltpu.VMEM)] * 3,
            out_specs=(pl.BlockSpec(memory_space=pl.ANY), pl.BlockSpec(memory_space=pltpu.VMEM)),
            scratch_shapes=[
                vm((3, NODES, LANES), F32),
                vm((NODES, LANES), F32),
                vm((NODES, LANES), jnp.int32),
                vm((NODES, LANES), jnp.int32),
                vm((3, NODES, LANES), F32),
                vm((NODES, LANES), F32),
                vm((7, NODES, LANES), F32),
                vm((64, LANES), F32),
                vm((2,) + tile, F32),
                vm((CELLS,) + tile, F32),
                vm((CELLS,) + tile, F32),
                vm((48, LANES), F32),
                vm((48, LANES // 4), F32),
                vm((2,) + tile, F32),
                vm((2,) + tile, F32),
                vm((NEWTON, 2, 3) + tile, F32),
                vm((NEWTON, 2, 3) + tile, F32),
                vm((4,) + tile, F32),
                vm((2,) + tile, F32),
                vm((2, 3) + tile, F32),
                vm((NEWTON + 1, 8, LANES), F32),
                vm((NEWTON + 1, 4, 1, LANES), F32),
                vm((NEWTON + 1, 4, 8, LANES), F32),
                vm((NEWTON + 1, 4, 1, LANES), F32),
                vm((3, SIDE, LANES), F32),
                vm((3, 8, LANES), F32),
                vm((3, 8, LANES), F32),
                vm((3, 8, LANES), F32),
                vm((8, LANES), F32),
                dma((3,)),
                dma,
                dma((NEWTON, 4)),
                dma((NEWTON, 4)),
                dma((4,)),
                dma((4,)),
                dma((NEWTON + 1, 4)),
                dma((NEWTON + 1, 4)),
                dma((NEWTON + 1, 4)),
                dma((NEWTON + 1, 4)),
            ],
            compiler_params=pltpu.CompilerParams(collective_id=0, has_side_effects=True),
        )
        state, warm = call(
            sol.reshape(3, NODES, LANES), ins.reshape(NODES, LANES), ele.reshape(NODES, LANES), imp, con, war
        )
        return state.reshape(3, SIDE, SIDE, LANES), warm

    spec = P("gx", "gy", None)
    return jax.shard_map(
        per_device,
        mesh=mesh,
        in_specs=(P(None, "gx", "gy", None),) + (spec,) * 5,
        out_specs=(P(None, "gx", "gy", None), spec),
        check_vma=False,
    )
```

```python
import functools

import jax
import jax.numpy as jnp
from jax import lax
from jax.experimental import pallas as pl
from jax.experimental.pallas import tpu as pltpu
from jax.sharding import PartitionSpec as P

NEWTON = 3
SWEEPS = 3
SIDE = 16
LANES = 128
CELLS = 4
NODES = SIDE * SIDE

CHARGE = 4.0
SHIFT = 24.0
BIAS = 0.25
HEAT_GAIN = 1.0
SINK = 0.3
DROP = 0.5

F32 = jnp.float32
MESH = pl.DeviceIdType.MESH
OPPOSITE = (1, 0, 3, 2)
DIAGONAL_OPPOSITE = (3, 2, 1, 0)


def face(pi, ni, qi, pj, nj, qj):
    d = pj - pi
    u = jnp.abs(d)
    v = d * d
    small = u < 0.5
    r = 1.0 / (jnp.exp(u) - 1.0)
    wide = u * r
    g_near = 1.0 + v * (1.0 / 12.0 + v * (-1.0 / 720.0 + v * (1.0 / 30240.0 + v * (-1.0 / 1209600.0))))
    h_near = u * (1.0 / 6.0 + v * (-1.0 / 180.0 + v * (1.0 / 5040.0 + v * (-1.0 / 151200.0))))
    b = jnp.where(small, g_near - 0.5 * u, wide)
    h = jnp.where(small, h_near, r * (1.0 - wide) - wide + 0.5)
    g = b + 0.5 * u
    h = jnp.where(d < 0.0, -h, h)
    plus = b + jnp.maximum(-d, 0.0)
    minus = b + jnp.maximum(d, 0.0)
    je = nj * plus - ni * minus
    jh = qj * minus - qi * plus
    gn = 0.5 * (nj + ni) - h * (nj - ni)
    gp = -0.5 * (qj + qi) - h * (qj - qi)
    return d, je, jh, gn, gp, g


def spread(a, lane):
    a = a + jnp.where((lane & 1) == 0, pltpu.roll(a, LANES - 1, 1), pltpu.roll(a, 1, 1))
    return a + jnp.where((lane & 2) == 0, pltpu.roll(a, LANES - 2, 1), pltpu.roll(a, 2, 1))


def body(
    nx, ny,
    sol_ref, ins_ref, ele_ref, imp_ref, con_ref, war_ref,
    out_ref, temp_ref,
    st, eps, ins, ele, imp, con, war, wl, fc, acc, hs, yq, mob, dop, moby, dopy, rep, small, wbx, wby,
    hx, hy, hex_, se, sy, ts, ds, tr, dr, tx, sx, cx, ix, dd,
    load_sem, store_sem, s_send, s_recv, e_send, e_recv, t_send, t_recv, d_send, d_recv,
):
    gx = lax.axis_index("gx")
    gy = lax.axis_index("gy")
    xl, xh = lax.rem(gx + nx - 1, nx), lax.rem(gx + 1, nx)
    yl, yh = lax.rem(gy + ny - 1, ny), lax.rem(gy + 1, ny)
    near = ((xl, gy), (xh, gy), (gx, yl), (gx, yh))
    corner = ((xl, yl), (xl, yh), (xh, yl), (xh, yh))
    has = (gx > 0, gx < nx - 1, gy > 0, gy < ny - 1)
    has_corner = (has[0] & has[2], has[0] & has[3], has[1] & has[2], has[1] & has[3])

    barrier = pltpu.get_barrier_semaphore()
    for s in (2, 3, 0, 1):

        @pl.when(has[s])
        def _():
            pl.semaphore_signal(barrier, inc=1, device_id=near[s], device_id_type=MESH)

    loads = [
        pltpu.make_async_copy(sol_ref, st, load_sem.at[0]),
        pltpu.make_async_copy(ins_ref, ins, load_sem.at[1]),
        pltpu.make_async_copy(imp_ref, imp, load_sem.at[2]),
        pltpu.make_async_copy(con_ref, con, load_sem.at[3]),
        pltpu.make_async_copy(war_ref, war, load_sem.at[4]),
        pltpu.make_async_copy(ele_ref, ele, load_sem.at[5]),
    ]
    for copy in loads:
        copy.start()

    lane = lax.broadcasted_iota(jnp.int32, (1, LANES), 1)
    lane4 = lane & 3
    last_lane = (lane != LANES - 1).astype(F32)
    last_row = (lax.broadcasted_iota(jnp.int32, (SIDE, LANES), 0) != SIDE - 1).astype(F32)

    def slab(x):
        return pl.ds(pl.multiple_of(x * SIDE, SIDE), SIDE)

    def remote(src, dst, send, recv, target):
        return pltpu.make_async_remote_copy(
            src_ref=src, dst_ref=dst, send_sem=send, recv_sem=recv, device_id=target, device_id_type=MESH
        )

    def start(copies, flags, order):
        for s in order:

            @pl.when(flags[s])
            def _():
                copies[s].start()

    def wait_sent(copies, flags):
        for s in range(4):

            @pl.when(flags[s])
            def _():
                copies[s].wait_send()

    def wait_arrived(copies, flags, opposite):
        for s in range(4):

            @pl.when(flags[s])
            def _():
                copies[opposite[s]].wait_recv()

    def state_copies(k):
        out = []
        for s in range(4):
            if s < 2:
                src = st.at[:, pl.ds(0 if s == 0 else NODES - SIDE, SIDE), :]
                dst = hx.at[k, OPPOSITE[s]]
            else:
                src, dst = sy.at[s - 2], hy.at[k, OPPOSITE[s] - 2]
            out.append(remote(src, dst, s_send.at[k, s], s_recv.at[k, OPPOSITE[s]], near[s]))
        return out

    def eps_copies():
        out = []
        for s in range(4):
            src = eps.at[pl.ds(0 if s == 0 else NODES - SIDE, SIDE), :] if s < 2 else se.at[s - 2]
            out.append(remote(src, hex_.at[OPPOSITE[s]], e_send.at[s], e_recv.at[OPPOSITE[s]], near[s]))
        return out

    def thermal_copies(t):
        sides, corners = [], []
        for s in range(4):
            o = OPPOSITE[s]
            sides.append(remote(ts.at[t], tr.at[t, o], t_send.at[t, s], t_recv.at[t, o], near[s]))
        for s in range(4):
            o = DIAGONAL_OPPOSITE[s]
            corners.append(remote(ds.at[t, s], dr.at[t, o], d_send.at[t, s], d_recv.at[t, o], corner[s]))
        return sides, corners

    def start_thermal(t):
        sides, corners = thermal_copies(t)
        start(corners, has_corner, range(4))
        start(sides, has, (2, 3, 0, 1))

    def wait_thermal(t):
        sides, corners = thermal_copies(t)
        wait_arrived(sides, has, OPPOSITE)
        wait_arrived(corners, has_corner, DIAGONAL_OPPOSITE)
        wait_sent(sides, has)
        wait_sent(corners, has_corner)

    def pack_rows():
        for f in range(3):
            sy[0, f] = st[f, pl.ds(0, SIDE, stride=SIDE), :]
            sy[1, f] = st[f, pl.ds(SIDE - 1, SIDE, stride=SIDE), :]

    def pack_thermal(t, warm, source):
        ts[t, 0:4, :] = warm
        ts[t, 4:8, :] = source
        tile = ts[t]
        up2, down2 = pltpu.roll(tile, 2, 1), pltpu.roll(tile, LANES - 2, 1)
        up3, down3 = pltpu.roll(tile, 3, 1), pltpu.roll(tile, LANES - 3, 1)

        def low(a, b):
            return jnp.where(lane4 < 2, tile[a:a + 1], jnp.where(lane4 == 2, up2[b:b + 1], up3[a + 4:a + 5]))

        def high(a, b):
            return jnp.where(lane4 >= 2, tile[a:a + 1], jnp.where(lane4 == 1, down2[b:b + 1], down3[a + 4:a + 5]))

        ds[t, 0] = low(0, 1)
        ds[t, 1] = high(0, 1)
        ds[t, 2] = low(3, 2)
        ds[t, 3] = high(3, 2)

    def keep(flag, a):
        return jnp.where(flag, a, jnp.zeros_like(a))

    def load_corners(t):
        for s in range(4):
            dd[s:s + 1, :] = keep(has_corner[s], dr[t, s])

    def gather_source(t, into):
        tile = dd[...]
        up3, down3 = pltpu.roll(tile, 3, 1), pltpu.roll(tile, LANES - 3, 1)
        into[1, 0:2, :] = keep(has[0], tr[t, 0, 6:8, :])
        into[1, 2:6, :] = ts[t, 4:8, :]
        into[1, 6:8, :] = keep(has[1], tr[t, 1, 4:6, :])
        into[0, 2:6, :] = keep(has[2], tr[t, 2, 4:8, :])
        into[2, 2:6, :] = keep(has[3], tr[t, 3, 4:8, :])
        into[0, 1:2, :] = up3[0:1]
        into[0, 6:7, :] = up3[2:3]
        into[2, 1:2, :] = down3[1:2]
        into[2, 6:7, :] = down3[3:4]

    def gather_warm(t):
        tile = dd[...]
        up2, down2 = pltpu.roll(tile, 2, 1), pltpu.roll(tile, LANES - 2, 1)
        tx[1, 0:3, :] = keep(has[0], tr[t, 0, 1:4, :])
        tx[1, 3:7, :] = ts[t, 0:4, :]
        tx[1, 7:10, :] = keep(has[1], tr[t, 1, 0:3, :])
        tx[0, 3:7, :] = keep(has[2], tr[t, 2, 0:4, :])
        tx[2, 3:7, :] = keep(has[3], tr[t, 3, 0:4, :])
        tx[0, 1:2, :] = up2[0:1]
        tx[0, 2:3, :] = tile[0:1]
        tx[0, 7:8, :] = tile[2:3]
        tx[0, 8:9, :] = up2[2:3]
        tx[2, 1:2, :] = down2[1:2]
        tx[2, 2:3, :] = tile[1:2]
        tx[2, 7:8, :] = tile[3:4]
        tx[2, 8:9, :] = down2[3:4]

    def relax(t):
        load_corners(t)
        gather_source(t, sx)
        gather_warm(t)
        for _ in range(SWEEPS):
            mid = [tx[b, 1:9, :] for b in range(3)]
            new = []
            for b in range(3):
                c = mid[b]
                z_low = jnp.where(lane >= 4, pltpu.roll(c, 4, 1), 0.0)
                z_high = jnp.where(lane < LANES - 4, pltpu.roll(c, LANES - 4, 1), 0.0)
                y_low, y_high = pltpu.roll(c, 1, 1), pltpu.roll(c, LANES - 1, 1)
                if b > 0:
                    y_low = jnp.where(lane4 > 0, y_low, pltpu.roll(mid[b - 1], LANES - 3, 1))
                if b < 2:
                    y_high = jnp.where(lane4 < 3, y_high, pltpu.roll(mid[b + 1], 3, 1))
                total = (tx[b, 0:8, :] + tx[b, 2:10, :]) + (y_low + y_high) + (z_low + z_high)
                new.append((sx[b] + cx[b] * total) * ix[b])
            for b in range(3):
                tx[b, 1:9, :] = new[b]
        return tx[1, 3:7, :]

    loads[0].wait()
    pack_rows()
    count = sum(flag.astype(jnp.int32) for flag in has)
    pl.semaphore_wait(barrier, count)
    start(state_copies(0), has, (2, 3, 0, 1))
    loads[1].wait()
    eps[...] = jnp.where(ins[...] == 1, 0.4, 1.0).astype(F32)
    se[0] = eps[pl.ds(0, SIDE, stride=SIDE), :]
    se[1] = eps[pl.ds(SIDE - 1, SIDE, stride=SIDE), :]
    start(eps_copies(), has, (2, 3, 0, 1))
    for copy in loads[2:]:
        copy.wait()

    def lookup(labels, table):
        result = jnp.zeros(labels.shape, F32)
        for level, amount in enumerate(table):
            result = jnp.where(labels == level, amount, result)
        return result

    for c in range(CELLS):
        small[4 * c:4 * c + 4, :] = lookup(imp[c], (-2.0, -0.5, 0.5, 2.0))
        small[16 + 4 * c:16 + 4 * c + 4, :] = lookup(con[c], (0.5, 1.0, 2.0, 4.0))
        small[32 + 4 * c:32 + 4 * c + 4, :] = war[c]
    zc = LANES // 4
    wide = (lax.broadcasted_iota(jnp.int32, (zc, LANES), 1) // 4 == lax.broadcasted_iota(jnp.int32, (zc, LANES), 0)).astype(F32)
    rep[...] = jnp.dot(small[...], wide, precision=lax.Precision.HIGHEST, preferred_element_type=F32)
    for c in range(CELLS):
        for y in range(CELLS):
            row = jnp.broadcast_to(rep[4 * c + y:4 * c + y + 1, :], (4, LANES))
            dop[c, 4 * y:4 * y + 4, :] = row
            if y in (0, CELLS - 1):
                dopy[y // (CELLS - 1), 4 * c:4 * c + 4, :] = row

    def packed(first):
        rows = [rep[pl.ds(first + y, 4, stride=4), :] for y in range(CELLS)]
        return jnp.where(lane4 == 0, rows[0], jnp.where(lane4 == 1, rows[1], jnp.where(lane4 == 2, rows[2], rows[3])))

    cond, warm0 = packed(16), packed(32)
    pack_thermal(0, cond, cond)
    ts[1, 0:4, :] = warm0
    tx[...] = jnp.zeros_like(tx)
    sx[...] = jnp.zeros_like(sx)
    cx[...] = jnp.zeros_like(cx)
    dd[...] = jnp.zeros_like(dd)

    def weigh(x, below, upper):
        e = eps[slab(x), :]
        wy = (e + pltpu.roll(e, SIDE - 1, 0)) * last_row
        wz = (e + pltpu.roll(e, LANES - 1, 1)) * last_lane
        wl[1, slab(x), :] = wy
        wl[2, slab(x), :] = wz
        total = below + wy + pltpu.roll(wy, 1, 0) + wz + pltpu.roll(wz, 1, 1)
        if not upper:
            fc[slab(x), :] = total
            return below
        wx = e + eps[slab(x + 1), :]
        wl[0, slab(x), :] = wx
        fc[slab(x), :] = total + wx
        return wx

    zero = jnp.zeros((SIDE, LANES), F32)
    below = lax.fori_loop(0, SIDE - 1, lambda x, b: weigh(x, b, True), zero)
    weigh(SIDE - 1, below, False)

    def fluxes(x, below, upper):
        psi, n, p = (st[f, slab(x), :] for f in range(3))
        d, je, jh, gn, gp, g = face(psi, n, p, *(pltpu.roll(a, SIDE - 1, 0) for a in (psi, n, p)))
        je, jh, gn, gp, g, ld = (a * last_row for a in (je, jh, gn, gp, g, d))
        lap = wl[1, slab(x), :] * d
        t = je - jh
        sums = [je, jh, lap, ld, gn, gp, g, t * t]
        sums = [a - pltpu.roll(a, 1, 0) if i < 4 else a + pltpu.roll(a, 1, 0) for i, a in enumerate(sums)]
        d, je, jh, gn, gp, g = face(psi, n, p, *(pltpu.roll(a, LANES - 1, 1) for a in (psi, n, p)))
        je, jh, gn, gp, g, ld = (a * last_lane for a in (je, jh, gn, gp, g, d))
        lap = wl[2, slab(x), :] * d
        t = je - jh
        more = [je, jh, lap, ld, gn, gp, g, t * t]
        more = [a - pltpu.roll(a, 1, 1) if i < 4 else a + pltpu.roll(a, 1, 1) for i, a in enumerate(more)]
        sums = [a + b for a, b in zip(sums, more)]
        sums = [a - b if i < 4 else a + b for i, (a, b) in enumerate(zip(sums, below))]
        carry = below
        if upper:
            d, je, jh, gn, gp, g = face(psi, n, p, *(st[f, slab(x + 1), :] for f in range(3)))
            t = je - jh
            carry = (je, jh, wl[0, slab(x), :] * d, d, gn, gp, g, t * t)
            sums = [a + b for a, b in zip(sums, carry)]
        for q in range(7):
            acc[q, slab(x), :] = sums[q]
        cell = slab(x // CELLS)
        hs[cell, :] = hs[cell, :] + sums[7] / (n + p)
        return carry

    def edge(side, mine, halo, weight):
        scale = has[side].astype(F32)
        halo = [jnp.where(has[side], a, b) for a, b in zip(halo, mine)]
        if side % 2 == 0:
            d, je, jh, gn, gp, g = face(*halo, *mine)
            sign = -scale
        else:
            d, je, jh, gn, gp, g = face(*mine, *halo)
            sign = scale
        t = (je - jh) * scale
        return (je * sign, jh * sign, weight * d * sign, d * sign, gn * scale, gp * scale, g * scale), t * t

    def newton(state, sums, faces, mu, level, contact):
        psi, n, p = state
        fe, fh, lap, ls, gn, gp, gs = sums
        rd = 1.0 / (n + p + 2.0)
        rec = (n * p - 1.0) * rd
        rn, rp = (p + 1.0) * rd, (n + 1.0) * rd
        rn, rp = rn * rn, rp * rp
        r0 = lap + CHARGE * (p - n + level)
        r1 = mu * fe - rec
        r2 = mu * fh - rec
        aa = -faces
        ba, ca = mu * gn, mu * gp
        bb = -mu * (gs + 0.5 * ls) - rn - SHIFT
        cc = -mu * (gs - 0.5 * ls) - rp - SHIFT
        bc, cb = -rp, -rn
        c_aa = bb * cc - bc * cb
        c_ab = bc * ca - ba * cc
        c_ac = ba * cb - bb * ca
        inv = 1.0 / (aa * c_aa + CHARGE * (c_ac - c_ab))
        d0 = (c_aa * r0 + CHARGE * ((cb + cc) * r1 - (bc + bb) * r2)) * inv
        d1 = (c_ab * r0 + (aa * cc - CHARGE * ca) * r1 + (CHARGE * ba - aa * bc) * r2) * inv
        d2 = (c_ac * r0 - (CHARGE * ca + aa * cb) * r1 + (aa * bb + CHARGE * ba) * r2) * inv
        d0 = jnp.where(contact, psi - BIAS * level, d0)
        d1 = jnp.where(contact, n - 1.0, d1)
        d2 = jnp.where(contact, p - 1.0, d2)
        return psi - d0, n * jnp.exp(-d1 / n), p * jnp.exp(-d2 / p)

    def step(k, nothing):
        hs[...] = jnp.zeros_like(hs)
        none = (zero,) * 8
        below = lax.fori_loop(0, SIDE - 1, lambda x, b: fluxes(x, b, True), none)
        fluxes(SIDE - 1, below, False)

        @pl.when(k == 0)
        def _():
            wait_arrived(eps_copies(), has, OPPOSITE)
            wait_sent(eps_copies(), has)
            for s in range(2):
                rows = pl.ds(s * (NODES - SIDE), SIDE)
                wbx[s] = keep(has[s], eps[rows, :] + hex_[s])
                fc[rows, :] = fc[rows, :] + wbx[s]
            for s in range(2):
                rows = pl.ds(s * (SIDE - 1), SIDE, stride=SIDE)
                wby[s] = keep(has[2 + s], se[s] + hex_[2 + s])
                fc[rows, :] = fc[rows, :] + wby[s]

        @pl.when(k == 1)
        def _():
            wait_thermal(0)
            load_corners(0)
            gather_source(0, cx)
            ix[...] = 1.0 / (SINK + 6.0 * cx[...])

        @pl.when(k > 0)
        def _():
            wait_thermal(k)
            ts[k + 1, 0:4, :] = relax(k)

        warm = ts[k + 1, 0:4, :]
        m = 1.0 / (1.0 + DROP * warm)
        m4 = spread(jnp.concatenate([jnp.where(lane4 == y, m, 0.0) for y in range(CELLS)], 0), lane)
        rep[0:16, :] = m4
        for c in range(CELLS):
            for y in range(CELLS):
                row = jnp.broadcast_to(rep[4 * y + c:4 * y + c + 1, :], (4, LANES))
                mob[c, 4 * y:4 * y + 4, :] = row
                if y in (0, CELLS - 1):
                    moby[y // (CELLS - 1), 4 * c:4 * c + 4, :] = row

        wait_arrived(state_copies(k), has, OPPOSITE)
        wait_sent(state_copies(k), has)
        for s in range(2):
            rows = pl.ds(s * (NODES - SIDE), SIDE)
            mine = [st[f, rows, :] for f in range(3)]
            sums, heat = edge(s, mine, [hx[k, s, f] for f in range(3)], wbx[s])
            for q in range(7):
                acc[q, rows, :] = acc[q, rows, :] + sums[q]
            cell = pl.ds(s * (64 - SIDE), SIDE)
            hs[cell, :] = hs[cell, :] + heat / (mine[1] + mine[2])
        for s in range(2):
            rows = pl.ds(s * (SIDE - 1), SIDE, stride=SIDE)
            mine = [sy[s, f] for f in range(3)]
            sums, heat = edge(2 + s, mine, [hy[k, s, f] for f in range(3)], wby[s])
            sums = [acc[q, rows, :] + sums[q] for q in range(7)]
            for q in range(7):
                acc[q, rows, :] = sums[q]
            yq[s] = heat / (mine[1] + mine[2])
            new = newton(mine, sums, fc[rows, :], moby[s], dopy[s], ele[rows, :] == 1)
            for f in range(3):
                sy[s, f] = new[f]

        following = jnp.minimum(k + 1, NEWTON - 1)

        @pl.when(k < NEWTON - 1)
        def _():
            start(state_copies(following), has, (2, 3))

        parts = []
        for y in range(CELLS):
            total = hs[pl.ds(4 * y, 4, stride=SIDE), :]
            for i in range(1, 4):
                total = total + hs[pl.ds(4 * y + i, 4, stride=SIDE), :]
            if y in (0, CELLS - 1):
                for i in range(4):
                    total = total + yq[y // (CELLS - 1), pl.ds(i, 4, stride=4), :]
            parts.append(total)
        rep[0:16, :] = spread(jnp.concatenate(parts, 0), lane)
        r = [rep[4 * y:4 * y + 4, :] for y in range(CELLS)]
        heat = jnp.where(lane4 == 0, r[0], jnp.where(lane4 == 1, r[1], jnp.where(lane4 == 2, r[2], r[3])))
        pack_thermal(k + 1, warm, heat * m * (HEAT_GAIN * 0.5 / 64.0))
        start_thermal(k + 1)

        def solve(x, nothing):
            rows = slab(x)
            cell = x // CELLS
            new = newton(
                [st[f, rows, :] for f in range(3)], [acc[q, rows, :] for q in range(7)],
                fc[rows, :], mob[cell], dop[cell], ele[rows, :] == 1,
            )
            for f in range(3):
                st[f, rows, :] = new[f]
            return nothing

        solve(0, 0)
        solve(SIDE - 1, 0)

        @pl.when(k < NEWTON - 1)
        def _():
            start(state_copies(following), has, (0, 1))

        @pl.when(k == 0)
        def _():
            start_thermal(0)

        lax.fori_loop(1, SIDE - 1, solve, 0)
        return nothing

    lax.fori_loop(0, NEWTON, step, 0)

    store = pltpu.make_async_copy(st, out_ref, store_sem)
    store.start()
    wait_thermal(NEWTON)
    warm = relax(NEWTON)
    cells = jnp.concatenate([jnp.where(lane4 == y, warm, 0.0) for y in range(CELLS)], 0)
    narrow = (lax.broadcasted_iota(jnp.int32, (LANES, zc), 0) // 4 == lax.broadcasted_iota(jnp.int32, (LANES, zc), 1)).astype(F32)
    cells = jnp.dot(cells, narrow, precision=lax.Precision.HIGHEST, preferred_element_type=F32)
    for c in range(CELLS):
        for y in range(CELLS):
            temp_ref[c, y:y + 1, :] = cells[4 * y + c:4 * y + c + 1, :]
    store.wait()


def solution(mesh):
    nx, ny = mesh.shape["gx"], mesh.shape["gy"]

    def per_device(sol, ins, ele, imp, con, war):
        vm = pltpu.VMEM
        dma = pltpu.SemaphoreType.DMA
        tile = (SIDE, LANES)
        call = pl.pallas_call(
            functools.partial(body, nx, ny),
            out_shape=(
                jax.ShapeDtypeStruct((3, NODES, LANES), F32),
                jax.ShapeDtypeStruct((CELLS, CELLS, LANES // 4), F32),
            ),
            in_specs=[pl.BlockSpec(memory_space=pl.ANY)] * 6,
            out_specs=(pl.BlockSpec(memory_space=pl.ANY), pl.BlockSpec(memory_space=pltpu.VMEM)),
            scratch_shapes=[
                vm((3, NODES, LANES), F32),
                vm((NODES, LANES), F32),
                vm((NODES, LANES), jnp.int32),
                vm((NODES, LANES), jnp.int32),
                vm((CELLS, CELLS, LANES // 4), jnp.int32),
                vm((CELLS, CELLS, LANES // 4), jnp.int32),
                vm((CELLS, CELLS, LANES // 4), F32),
                vm((3, NODES, LANES), F32),
                vm((NODES, LANES), F32),
                vm((7, NODES, LANES), F32),
                vm((64, LANES), F32),
                vm((2,) + tile, F32),
                vm((CELLS,) + tile, F32),
                vm((CELLS,) + tile, F32),
                vm((2,) + tile, F32),
                vm((2,) + tile, F32),
                vm((48, LANES), F32),
                vm((48, LANES // 4), F32),
                vm((2,) + tile, F32),
                vm((2,) + tile, F32),
                vm((NEWTON, 2, 3) + tile, F32),
                vm((NEWTON, 2, 3) + tile, F32),
                vm((4,) + tile, F32),
                vm((2,) + tile, F32),
                vm((2, 3) + tile, F32),
                vm((NEWTON + 1, 8, LANES), F32),
                vm((NEWTON + 1, 4, 1, LANES), F32),
                vm((NEWTON + 1, 4, 8, LANES), F32),
                vm((NEWTON + 1, 4, 1, LANES), F32),
                vm((3, SIDE, LANES), F32),
                vm((3, 8, LANES), F32),
                vm((3, 8, LANES), F32),
                vm((3, 8, LANES), F32),
                vm((8, LANES), F32),
                dma((6,)),
                dma,
                dma((NEWTON, 4)),
                dma((NEWTON, 4)),
                dma((4,)),
                dma((4,)),
                dma((NEWTON + 1, 4)),
                dma((NEWTON + 1, 4)),
                dma((NEWTON + 1, 4)),
                dma((NEWTON + 1, 4)),
            ],
            compiler_params=pltpu.CompilerParams(collective_id=0, has_side_effects=True),
        )
        state, warm = call(
            sol.reshape(3, NODES, LANES), ins.reshape(NODES, LANES), ele.reshape(NODES, LANES), imp, con, war
        )
        return state.reshape(3, SIDE, SIDE, LANES), warm

    spec = P("gx", "gy", None)
    return jax.shard_map(
        per_device,
        mesh=mesh,
        in_specs=(P(None, "gx", "gy", None),) + (spec,) * 5,
        out_specs=(P(None, "gx", "gy", None), spec),
        check_vma=False,
    )
```

```python
import functools

import jax
import jax.numpy as jnp
from jax import lax
from jax.experimental import pallas as pl
from jax.experimental.pallas import tpu as pltpu
from jax.sharding import PartitionSpec as P

NEWTON = 3
SWEEPS = 3
SIDE = 16
LANES = 128
CELLS = 4
NODES = SIDE * SIDE

CHARGE = 4.0
SHIFT = 24.0
BIAS = 0.25
HEAT_GAIN = 1.0
SINK = 0.3
DROP = 0.5

F32 = jnp.float32
MESH = pl.DeviceIdType.MESH
OPPOSITE = (1, 0, 3, 2)
DIAGONAL_OPPOSITE = (3, 2, 1, 0)


def face(pi, ni, qi, pj, nj, qj):
    d = pj - pi
    u = jnp.abs(d)
    v = d * d
    small = u < 0.5
    r = 1.0 / (jnp.exp(u) - 1.0)
    wide = u * r
    g_near = 1.0 + v * (1.0 / 12.0 + v * (-1.0 / 720.0 + v * (1.0 / 30240.0 + v * (-1.0 / 1209600.0))))
    h_near = u * (1.0 / 6.0 + v * (-1.0 / 180.0 + v * (1.0 / 5040.0 + v * (-1.0 / 151200.0))))
    b = jnp.where(small, g_near - 0.5 * u, wide)
    h = jnp.where(small, h_near, r * (1.0 - wide) - wide + 0.5)
    g = b + 0.5 * u
    h = jnp.where(d < 0.0, -h, h)
    plus = b + jnp.maximum(-d, 0.0)
    minus = b + jnp.maximum(d, 0.0)
    je = nj * plus - ni * minus
    jh = qj * minus - qi * plus
    gn = 0.5 * (nj + ni) - h * (nj - ni)
    gp = -0.5 * (qj + qi) - h * (qj - qi)
    return d, je, jh, gn, gp, g


def spread(a, lane):
    a = a + jnp.where((lane & 1) == 0, pltpu.roll(a, LANES - 1, 1), pltpu.roll(a, 1, 1))
    return a + jnp.where((lane & 2) == 0, pltpu.roll(a, LANES - 2, 1), pltpu.roll(a, 2, 1))


def body(
    nx, ny,
    sol_ref, ins_ref, ele_ref, imp_ref, con_ref, war_ref,
    st, temp_ref,
    eps, ins, ele, imp, con, war, wl, fc, acc, hs, yq, mob, dop, moby, dopy, rep, small, wbx, wby,
    hx, hy, hex_, se, sy, ts, ds, tr, dr, tx, sx, cx, ix, dd,
    load_sem, s_send, s_recv, e_send, e_recv, t_send, t_recv, d_send, d_recv,
):
    gx = lax.axis_index("gx")
    gy = lax.axis_index("gy")
    xl, xh = lax.rem(gx + nx - 1, nx), lax.rem(gx + 1, nx)
    yl, yh = lax.rem(gy + ny - 1, ny), lax.rem(gy + 1, ny)
    near = ((xl, gy), (xh, gy), (gx, yl), (gx, yh))
    corner = ((xl, yl), (xl, yh), (xh, yl), (xh, yh))
    has = (gx > 0, gx < nx - 1, gy > 0, gy < ny - 1)
    has_corner = (has[0] & has[2], has[0] & has[3], has[1] & has[2], has[1] & has[3])

    barrier = pltpu.get_barrier_semaphore()
    for s in (2, 3, 0, 1):

        @pl.when(has[s])
        def _():
            pl.semaphore_signal(barrier, inc=1, device_id=near[s], device_id_type=MESH)

    loads = [
        pltpu.make_async_copy(sol_ref, st, load_sem.at[0]),
        pltpu.make_async_copy(ins_ref, ins, load_sem.at[1]),
        pltpu.make_async_copy(imp_ref, imp, load_sem.at[2]),
        pltpu.make_async_copy(con_ref, con, load_sem.at[3]),
        pltpu.make_async_copy(war_ref, war, load_sem.at[4]),
        pltpu.make_async_copy(ele_ref, ele, load_sem.at[5]),
    ]
    for copy in loads:
        copy.start()

    lane = lax.broadcasted_iota(jnp.int32, (1, LANES), 1)
    lane4 = lane & 3
    last_lane = (lane != LANES - 1).astype(F32)
    last_row = (lax.broadcasted_iota(jnp.int32, (SIDE, LANES), 0) != SIDE - 1).astype(F32)

    def slab(x):
        return pl.ds(pl.multiple_of(x * SIDE, SIDE), SIDE)

    def remote(src, dst, send, recv, target):
        return pltpu.make_async_remote_copy(
            src_ref=src, dst_ref=dst, send_sem=send, recv_sem=recv, device_id=target, device_id_type=MESH
        )

    def start(copies, flags, order):
        for s in order:

            @pl.when(flags[s])
            def _():
                copies[s].start()

    def wait_sent(copies, flags):
        for s in range(4):

            @pl.when(flags[s])
            def _():
                copies[s].wait_send()

    def wait_arrived(copies, flags, opposite):
        for s in range(4):

            @pl.when(flags[s])
            def _():
                copies[opposite[s]].wait_recv()

    def state_copies(k):
        out = []
        for s in range(4):
            if s < 2:
                src = st.at[:, pl.ds(0 if s == 0 else NODES - SIDE, SIDE), :]
                dst = hx.at[k, OPPOSITE[s]]
            else:
                src, dst = sy.at[s - 2], hy.at[k, OPPOSITE[s] - 2]
            out.append(remote(src, dst, s_send.at[k, s], s_recv.at[k, OPPOSITE[s]], near[s]))
        return out

    def eps_copies():
        out = []
        for s in range(4):
            src = eps.at[pl.ds(0 if s == 0 else NODES - SIDE, SIDE), :] if s < 2 else se.at[s - 2]
            out.append(remote(src, hex_.at[OPPOSITE[s]], e_send.at[s], e_recv.at[OPPOSITE[s]], near[s]))
        return out

    def thermal_copies(t):
        sides, corners = [], []
        for s in range(4):
            o = OPPOSITE[s]
            sides.append(remote(ts.at[t], tr.at[t, o], t_send.at[t, s], t_recv.at[t, o], near[s]))
        for s in range(4):
            o = DIAGONAL_OPPOSITE[s]
            corners.append(remote(ds.at[t, s], dr.at[t, o], d_send.at[t, s], d_recv.at[t, o], corner[s]))
        return sides, corners

    def start_thermal(t):
        sides, corners = thermal_copies(t)
        start(corners, has_corner, range(4))
        start(sides, has, (2, 3, 0, 1))

    def wait_thermal(t):
        sides, corners = thermal_copies(t)
        wait_arrived(sides, has, OPPOSITE)
        wait_arrived(corners, has_corner, DIAGONAL_OPPOSITE)
        wait_sent(sides, has)
        wait_sent(corners, has_corner)

    def pack_rows():
        for f in range(3):
            sy[0, f] = st[f, pl.ds(0, SIDE, stride=SIDE), :]
            sy[1, f] = st[f, pl.ds(SIDE - 1, SIDE, stride=SIDE), :]

    def pack_thermal(t, warm, source):
        ts[t, 0:4, :] = warm
        ts[t, 4:8, :] = source
        tile = ts[t]
        up2, down2 = pltpu.roll(tile, 2, 1), pltpu.roll(tile, LANES - 2, 1)
        up3, down3 = pltpu.roll(tile, 3, 1), pltpu.roll(tile, LANES - 3, 1)

        def low(a, b):
            return jnp.where(lane4 < 2, tile[a:a + 1], jnp.where(lane4 == 2, up2[b:b + 1], up3[a + 4:a + 5]))

        def high(a, b):
            return jnp.where(lane4 >= 2, tile[a:a + 1], jnp.where(lane4 == 1, down2[b:b + 1], down3[a + 4:a + 5]))

        ds[t, 0] = low(0, 1)
        ds[t, 1] = high(0, 1)
        ds[t, 2] = low(3, 2)
        ds[t, 3] = high(3, 2)

    def keep(flag, a):
        return jnp.where(flag, a, jnp.zeros_like(a))

    def load_corners(t):
        for s in range(4):
            dd[s:s + 1, :] = keep(has_corner[s], dr[t, s])

    def gather_source(t, into):
        tile = dd[...]
        up3, down3 = pltpu.roll(tile, 3, 1), pltpu.roll(tile, LANES - 3, 1)
        into[1, 0:2, :] = keep(has[0], tr[t, 0, 6:8, :])
        into[1, 2:6, :] = ts[t, 4:8, :]
        into[1, 6:8, :] = keep(has[1], tr[t, 1, 4:6, :])
        into[0, 2:6, :] = keep(has[2], tr[t, 2, 4:8, :])
        into[2, 2:6, :] = keep(has[3], tr[t, 3, 4:8, :])
        into[0, 1:2, :] = up3[0:1]
        into[0, 6:7, :] = up3[2:3]
        into[2, 1:2, :] = down3[1:2]
        into[2, 6:7, :] = down3[3:4]

    def gather_warm(t):
        tile = dd[...]
        up2, down2 = pltpu.roll(tile, 2, 1), pltpu.roll(tile, LANES - 2, 1)
        tx[1, 0:3, :] = keep(has[0], tr[t, 0, 1:4, :])
        tx[1, 3:7, :] = ts[t, 0:4, :]
        tx[1, 7:10, :] = keep(has[1], tr[t, 1, 0:3, :])
        tx[0, 3:7, :] = keep(has[2], tr[t, 2, 0:4, :])
        tx[2, 3:7, :] = keep(has[3], tr[t, 3, 0:4, :])
        tx[0, 1:2, :] = up2[0:1]
        tx[0, 2:3, :] = tile[0:1]
        tx[0, 7:8, :] = tile[2:3]
        tx[0, 8:9, :] = up2[2:3]
        tx[2, 1:2, :] = down2[1:2]
        tx[2, 2:3, :] = tile[1:2]
        tx[2, 7:8, :] = tile[3:4]
        tx[2, 8:9, :] = down2[3:4]

    def relax(t):
        load_corners(t)
        gather_source(t, sx)
        gather_warm(t)
        for _ in range(SWEEPS):
            mid = [tx[b, 1:9, :] for b in range(3)]
            new = []
            for b in range(3):
                c = mid[b]
                z_low = jnp.where(lane >= 4, pltpu.roll(c, 4, 1), 0.0)
                z_high = jnp.where(lane < LANES - 4, pltpu.roll(c, LANES - 4, 1), 0.0)
                y_low, y_high = pltpu.roll(c, 1, 1), pltpu.roll(c, LANES - 1, 1)
                if b > 0:
                    y_low = jnp.where(lane4 > 0, y_low, pltpu.roll(mid[b - 1], LANES - 3, 1))
                if b < 2:
                    y_high = jnp.where(lane4 < 3, y_high, pltpu.roll(mid[b + 1], 3, 1))
                total = (tx[b, 0:8, :] + tx[b, 2:10, :]) + (y_low + y_high) + (z_low + z_high)
                new.append((sx[b] + cx[b] * total) * ix[b])
            for b in range(3):
                tx[b, 1:9, :] = new[b]
        return tx[1, 3:7, :]

    loads[0].wait()
    pack_rows()
    count = sum(flag.astype(jnp.int32) for flag in has)
    pl.semaphore_wait(barrier, count)
    start(state_copies(0), has, (2, 3, 0, 1))
    loads[1].wait()
    eps[...] = jnp.where(ins[...] == 1, 0.4, 1.0).astype(F32)
    se[0] = eps[pl.ds(0, SIDE, stride=SIDE), :]
    se[1] = eps[pl.ds(SIDE - 1, SIDE, stride=SIDE), :]
    start(eps_copies(), has, (2, 3, 0, 1))
    for copy in loads[2:]:
        copy.wait()

    def lookup(labels, table):
        result = jnp.zeros(labels.shape, F32)
        for level, amount in enumerate(table):
            result = jnp.where(labels == level, amount, result)
        return result

    for c in range(CELLS):
        small[4 * c:4 * c + 4, :] = lookup(imp[c], (-2.0, -0.5, 0.5, 2.0))
        small[16 + 4 * c:16 + 4 * c + 4, :] = lookup(con[c], (0.5, 1.0, 2.0, 4.0))
        small[32 + 4 * c:32 + 4 * c + 4, :] = war[c]
    zc = LANES // 4
    wide = (lax.broadcasted_iota(jnp.int32, (zc, LANES), 1) // 4 == lax.broadcasted_iota(jnp.int32, (zc, LANES), 0)).astype(F32)
    rep[...] = jnp.dot(small[...], wide, precision=lax.Precision.HIGHEST, preferred_element_type=F32)
    for c in range(CELLS):
        for y in range(CELLS):
            row = jnp.broadcast_to(rep[4 * c + y:4 * c + y + 1, :], (4, LANES))
            dop[c, 4 * y:4 * y + 4, :] = row
            if y in (0, CELLS - 1):
                dopy[y // (CELLS - 1), 4 * c:4 * c + 4, :] = row

    def packed(first):
        rows = [rep[pl.ds(first + y, 4, stride=4), :] for y in range(CELLS)]
        return jnp.where(lane4 == 0, rows[0], jnp.where(lane4 == 1, rows[1], jnp.where(lane4 == 2, rows[2], rows[3])))

    cond, warm0 = packed(16), packed(32)
    pack_thermal(0, cond, cond)
    ts[1, 0:4, :] = warm0
    tx[...] = jnp.zeros_like(tx)
    sx[...] = jnp.zeros_like(sx)
    cx[...] = jnp.zeros_like(cx)
    dd[...] = jnp.zeros_like(dd)

    def weigh(x, below, upper):
        e = eps[slab(x), :]
        wy = (e + pltpu.roll(e, SIDE - 1, 0)) * last_row
        wz = (e + pltpu.roll(e, LANES - 1, 1)) * last_lane
        wl[1, slab(x), :] = wy
        wl[2, slab(x), :] = wz
        total = below + wy + pltpu.roll(wy, 1, 0) + wz + pltpu.roll(wz, 1, 1)
        if not upper:
            fc[slab(x), :] = total
            return below
        wx = e + eps[slab(x + 1), :]
        wl[0, slab(x), :] = wx
        fc[slab(x), :] = total + wx
        return wx

    zero = jnp.zeros((SIDE, LANES), F32)
    below = lax.fori_loop(0, SIDE - 1, lambda x, b: weigh(x, b, True), zero)
    weigh(SIDE - 1, below, False)

    def fluxes(x, below, upper):
        psi, n, p = (st[f, slab(x), :] for f in range(3))
        d, je, jh, gn, gp, g = face(psi, n, p, *(pltpu.roll(a, SIDE - 1, 0) for a in (psi, n, p)))
        je, jh, gn, gp, g, ld = (a * last_row for a in (je, jh, gn, gp, g, d))
        lap = wl[1, slab(x), :] * d
        t = je - jh
        sums = [je, jh, lap, ld, gn, gp, g, t * t]
        sums = [a - pltpu.roll(a, 1, 0) if i < 4 else a + pltpu.roll(a, 1, 0) for i, a in enumerate(sums)]
        d, je, jh, gn, gp, g = face(psi, n, p, *(pltpu.roll(a, LANES - 1, 1) for a in (psi, n, p)))
        je, jh, gn, gp, g, ld = (a * last_lane for a in (je, jh, gn, gp, g, d))
        lap = wl[2, slab(x), :] * d
        t = je - jh
        more = [je, jh, lap, ld, gn, gp, g, t * t]
        more = [a - pltpu.roll(a, 1, 1) if i < 4 else a + pltpu.roll(a, 1, 1) for i, a in enumerate(more)]
        sums = [a + b for a, b in zip(sums, more)]
        sums = [a - b if i < 4 else a + b for i, (a, b) in enumerate(zip(sums, below))]
        carry = below
        if upper:
            d, je, jh, gn, gp, g = face(psi, n, p, *(st[f, slab(x + 1), :] for f in range(3)))
            t = je - jh
            carry = (je, jh, wl[0, slab(x), :] * d, d, gn, gp, g, t * t)
            sums = [a + b for a, b in zip(sums, carry)]
        for q in range(7):
            acc[q, slab(x), :] = sums[q]
        cell = slab(x // CELLS)
        hs[cell, :] = hs[cell, :] + sums[7] / (n + p)
        return carry

    def edge(side, mine, halo, weight):
        scale = has[side].astype(F32)
        halo = [jnp.where(has[side], a, b) for a, b in zip(halo, mine)]
        if side % 2 == 0:
            d, je, jh, gn, gp, g = face(*halo, *mine)
            sign = -scale
        else:
            d, je, jh, gn, gp, g = face(*mine, *halo)
            sign = scale
        t = (je - jh) * scale
        return (je * sign, jh * sign, weight * d * sign, d * sign, gn * scale, gp * scale, g * scale), t * t

    def newton(state, sums, faces, mu, level, contact):
        psi, n, p = state
        fe, fh, lap, ls, gn, gp, gs = sums
        rd = 1.0 / (n + p + 2.0)
        rec = (n * p - 1.0) * rd
        rn, rp = (p + 1.0) * rd, (n + 1.0) * rd
        rn, rp = rn * rn, rp * rp
        r0 = lap + CHARGE * (p - n + level)
        r1 = mu * fe - rec
        r2 = mu * fh - rec
        aa = -faces
        ba, ca = mu * gn, mu * gp
        bb = -mu * (gs + 0.5 * ls) - rn - SHIFT
        cc = -mu * (gs - 0.5 * ls) - rp - SHIFT
        bc, cb = -rp, -rn
        c_aa = bb * cc - bc * cb
        c_ab = bc * ca - ba * cc
        c_ac = ba * cb - bb * ca
        inv = 1.0 / (aa * c_aa + CHARGE * (c_ac - c_ab))
        d0 = (c_aa * r0 + CHARGE * ((cb + cc) * r1 - (bc + bb) * r2)) * inv
        d1 = (c_ab * r0 + (aa * cc - CHARGE * ca) * r1 + (CHARGE * ba - aa * bc) * r2) * inv
        d2 = (c_ac * r0 - (CHARGE * ca + aa * cb) * r1 + (aa * bb + CHARGE * ba) * r2) * inv
        d0 = jnp.where(contact, psi - BIAS * level, d0)
        d1 = jnp.where(contact, n - 1.0, d1)
        d2 = jnp.where(contact, p - 1.0, d2)
        return psi - d0, n * jnp.exp(-d1 / n), p * jnp.exp(-d2 / p)

    def step(k, nothing):
        hs[...] = jnp.zeros_like(hs)
        none = (zero,) * 8
        below = lax.fori_loop(0, SIDE - 1, lambda x, b: fluxes(x, b, True), none)
        fluxes(SIDE - 1, below, False)

        @pl.when(k == 0)
        def _():
            wait_arrived(eps_copies(), has, OPPOSITE)
            wait_sent(eps_copies(), has)
            for s in range(2):
                rows = pl.ds(s * (NODES - SIDE), SIDE)
                wbx[s] = keep(has[s], eps[rows, :] + hex_[s])
                fc[rows, :] = fc[rows, :] + wbx[s]
            for s in range(2):
                rows = pl.ds(s * (SIDE - 1), SIDE, stride=SIDE)
                wby[s] = keep(has[2 + s], se[s] + hex_[2 + s])
                fc[rows, :] = fc[rows, :] + wby[s]

        @pl.when(k == 1)
        def _():
            wait_thermal(0)
            load_corners(0)
            gather_source(0, cx)
            ix[...] = 1.0 / (SINK + 6.0 * cx[...])

        @pl.when(k > 0)
        def _():
            wait_thermal(k)
            ts[k + 1, 0:4, :] = relax(k)

        warm = ts[k + 1, 0:4, :]
        m = 1.0 / (1.0 + DROP * warm)
        m4 = spread(jnp.concatenate([jnp.where(lane4 == y, m, 0.0) for y in range(CELLS)], 0), lane)
        rep[0:16, :] = m4
        for c in range(CELLS):
            for y in range(CELLS):
                row = jnp.broadcast_to(rep[4 * y + c:4 * y + c + 1, :], (4, LANES))
                mob[c, 4 * y:4 * y + 4, :] = row
                if y in (0, CELLS - 1):
                    moby[y // (CELLS - 1), 4 * c:4 * c + 4, :] = row

        wait_arrived(state_copies(k), has, OPPOSITE)
        wait_sent(state_copies(k), has)
        for s in range(2):
            rows = pl.ds(s * (NODES - SIDE), SIDE)
            mine = [st[f, rows, :] for f in range(3)]
            sums, heat = edge(s, mine, [hx[k, s, f] for f in range(3)], wbx[s])
            for q in range(7):
                acc[q, rows, :] = acc[q, rows, :] + sums[q]
            cell = pl.ds(s * (64 - SIDE), SIDE)
            hs[cell, :] = hs[cell, :] + heat / (mine[1] + mine[2])
        for s in range(2):
            rows = pl.ds(s * (SIDE - 1), SIDE, stride=SIDE)
            mine = [sy[s, f] for f in range(3)]
            sums, heat = edge(2 + s, mine, [hy[k, s, f] for f in range(3)], wby[s])
            sums = [acc[q, rows, :] + sums[q] for q in range(7)]
            for q in range(7):
                acc[q, rows, :] = sums[q]
            yq[s] = heat / (mine[1] + mine[2])
            new = newton(mine, sums, fc[rows, :], moby[s], dopy[s], ele[rows, :] == 1)
            for f in range(3):
                sy[s, f] = new[f]

        following = jnp.minimum(k + 1, NEWTON - 1)

        @pl.when(k < NEWTON - 1)
        def _():
            start(state_copies(following), has, (2, 3))

        parts = []
        for y in range(CELLS):
            total = hs[pl.ds(4 * y, 4, stride=SIDE), :]
            for i in range(1, 4):
                total = total + hs[pl.ds(4 * y + i, 4, stride=SIDE), :]
            if y in (0, CELLS - 1):
                for i in range(4):
                    total = total + yq[y // (CELLS - 1), pl.ds(i, 4, stride=4), :]
            parts.append(total)
        rep[0:16, :] = spread(jnp.concatenate(parts, 0), lane)
        r = [rep[4 * y:4 * y + 4, :] for y in range(CELLS)]
        heat = jnp.where(lane4 == 0, r[0], jnp.where(lane4 == 1, r[1], jnp.where(lane4 == 2, r[2], r[3])))
        pack_thermal(k + 1, warm, heat * m * (HEAT_GAIN * 0.5 / 64.0))
        start_thermal(k + 1)

        def solve(x, nothing):
            rows = slab(x)
            cell = x // CELLS
            new = newton(
                [st[f, rows, :] for f in range(3)], [acc[q, rows, :] for q in range(7)],
                fc[rows, :], mob[cell], dop[cell], ele[rows, :] == 1,
            )
            for f in range(3):
                st[f, rows, :] = new[f]
            return nothing

        solve(0, 0)
        solve(SIDE - 1, 0)

        @pl.when(k < NEWTON - 1)
        def _():
            start(state_copies(following), has, (0, 1))

        @pl.when(k == 0)
        def _():
            start_thermal(0)

        lax.fori_loop(1, SIDE - 1, solve, 0)
        return nothing

    lax.fori_loop(0, NEWTON, step, 0)

    wait_thermal(NEWTON)
    temp_ref[0:4, :] = relax(NEWTON)


def emit(st_ref, warm_ref, out_ref, temp_ref, sem):
    store = pltpu.make_async_copy(st_ref, out_ref, sem)
    store.start()
    warm = warm_ref[0:4, :]
    lane4 = lax.broadcasted_iota(jnp.int32, (1, LANES), 1) & 3
    zc = LANES // 4
    cells = jnp.concatenate([jnp.where(lane4 == y, warm, 0.0) for y in range(CELLS)], 0)
    narrow = (lax.broadcasted_iota(jnp.int32, (LANES, zc), 0) // 4 == lax.broadcasted_iota(jnp.int32, (LANES, zc), 1)).astype(F32)
    cells = jnp.dot(cells, narrow, precision=lax.Precision.HIGHEST, preferred_element_type=F32)
    for c in range(CELLS):
        for y in range(CELLS):
            temp_ref[c, y:y + 1, :] = cells[4 * y + c:4 * y + c + 1, :]
    store.wait()


def solution(mesh):
    nx, ny = mesh.shape["gx"], mesh.shape["gy"]

    def per_device(sol, ins, ele, imp, con, war):
        vm = pltpu.VMEM
        dma = pltpu.SemaphoreType.DMA
        tile = (SIDE, LANES)
        call = pl.pallas_call(
            functools.partial(body, nx, ny),
            out_shape=(
                pltpu.VMEM((3, NODES, LANES), F32),
                pltpu.VMEM((8, LANES), F32),
            ),
            in_specs=[pl.BlockSpec(memory_space=pl.ANY)] * 6,
            out_specs=(pl.BlockSpec(memory_space=pltpu.VMEM), pl.BlockSpec(memory_space=pltpu.VMEM)),
            scratch_shapes=[
                vm((NODES, LANES), F32),
                vm((NODES, LANES), jnp.int32),
                vm((NODES, LANES), jnp.int32),
                vm((CELLS, CELLS, LANES // 4), jnp.int32),
                vm((CELLS, CELLS, LANES // 4), jnp.int32),
                vm((CELLS, CELLS, LANES // 4), F32),
                vm((3, NODES, LANES), F32),
                vm((NODES, LANES), F32),
                vm((7, NODES, LANES), F32),
                vm((64, LANES), F32),
                vm((2,) + tile, F32),
                vm((CELLS,) + tile, F32),
                vm((CELLS,) + tile, F32),
                vm((2,) + tile, F32),
                vm((2,) + tile, F32),
                vm((48, LANES), F32),
                vm((48, LANES // 4), F32),
                vm((2,) + tile, F32),
                vm((2,) + tile, F32),
                vm((NEWTON, 2, 3) + tile, F32),
                vm((NEWTON, 2, 3) + tile, F32),
                vm((4,) + tile, F32),
                vm((2,) + tile, F32),
                vm((2, 3) + tile, F32),
                vm((NEWTON + 1, 8, LANES), F32),
                vm((NEWTON + 1, 4, 1, LANES), F32),
                vm((NEWTON + 1, 4, 8, LANES), F32),
                vm((NEWTON + 1, 4, 1, LANES), F32),
                vm((3, SIDE, LANES), F32),
                vm((3, 8, LANES), F32),
                vm((3, 8, LANES), F32),
                vm((3, 8, LANES), F32),
                vm((8, LANES), F32),
                dma((6,)),
                dma((NEWTON, 4)),
                dma((NEWTON, 4)),
                dma((4,)),
                dma((4,)),
                dma((NEWTON + 1, 4)),
                dma((NEWTON + 1, 4)),
                dma((NEWTON + 1, 4)),
                dma((NEWTON + 1, 4)),
            ],
            compiler_params=pltpu.CompilerParams(collective_id=0, has_side_effects=True),
        )
        state, warm = call(
            sol.reshape(3, NODES, LANES), ins.reshape(NODES, LANES), ele.reshape(NODES, LANES), imp, con, war
        )
        state = pltpu.with_memory_space_constraint(state, pltpu.VMEM)
        warm = pltpu.with_memory_space_constraint(warm, pltpu.VMEM)
        state, warm = pl.pallas_call(
            emit,
            out_shape=(
                jax.ShapeDtypeStruct((3, NODES, LANES), F32),
                jax.ShapeDtypeStruct((CELLS, CELLS, LANES // 4), F32),
            ),
            in_specs=[pl.BlockSpec(memory_space=pltpu.VMEM), pl.BlockSpec(memory_space=pltpu.VMEM)],
            out_specs=(pl.BlockSpec(memory_space=pl.ANY), pl.BlockSpec(memory_space=pltpu.VMEM)),
            scratch_shapes=[dma],
        )(state, warm)
        return state.reshape(3, SIDE, SIDE, LANES), warm

    spec = P("gx", "gy", None)
    return jax.shard_map(
        per_device,
        mesh=mesh,
        in_specs=(P(None, "gx", "gy", None),) + (spec,) * 5,
        out_specs=(P(None, "gx", "gy", None), spec),
        check_vma=False,
    )
```

```python
import functools

import jax
import jax.numpy as jnp
from jax import lax
from jax.experimental import pallas as pl
from jax.experimental.pallas import tpu as pltpu
from jax.sharding import PartitionSpec as P

NEWTON = 3
SWEEPS = 3
SIDE = 16
LANES = 128
CELLS = 4
NODES = SIDE * SIDE

CHARGE = 4.0
SHIFT = 24.0
BIAS = 0.25
HEAT_GAIN = 1.0
SINK = 0.3
DROP = 0.5

F32 = jnp.float32
MESH = pl.DeviceIdType.MESH
OPPOSITE = (1, 0, 3, 2)
DIAGONAL_OPPOSITE = (3, 2, 1, 0)


def face(pi, ni, qi, pj, nj, qj):
    d = pj - pi
    u = jnp.abs(d)
    v = d * d
    small = u < 0.5
    r = 1.0 / (jnp.exp(u) - 1.0)
    wide = u * r
    g_near = 1.0 + v * (1.0 / 12.0 + v * (-1.0 / 720.0 + v * (1.0 / 30240.0 + v * (-1.0 / 1209600.0))))
    h_near = u * (1.0 / 6.0 + v * (-1.0 / 180.0 + v * (1.0 / 5040.0 + v * (-1.0 / 151200.0))))
    b = jnp.where(small, g_near - 0.5 * u, wide)
    h = jnp.where(small, h_near, r * (1.0 - wide) - wide + 0.5)
    g = b + 0.5 * u
    h = jnp.where(d < 0.0, -h, h)
    plus = b + jnp.maximum(-d, 0.0)
    minus = b + jnp.maximum(d, 0.0)
    je = nj * plus - ni * minus
    jh = qj * minus - qi * plus
    gn = 0.5 * (nj + ni) - h * (nj - ni)
    gp = -0.5 * (qj + qi) - h * (qj - qi)
    return d, je, jh, gn, gp, g


def spread(a, lane):
    a = a + jnp.where((lane & 1) == 0, pltpu.roll(a, LANES - 1, 1), pltpu.roll(a, 1, 1))
    return a + jnp.where((lane & 2) == 0, pltpu.roll(a, LANES - 2, 1), pltpu.roll(a, 2, 1))


def body(
    nx, ny,
    sol_ref, ins_ref, ele_ref, imp_ref, con_ref, war_ref,
    st, temp_ref,
    eps, ins, ele, imp, con, war, wl, fc, acc, hs, qe, hin, mob, dop, mobb, dopb, fcb, eleb, rep, small, wb,
    hb, hex_, se, sb, cs, cr, ts, ds, tr, dr, tx, sx, cx, ix, dd,
    load_sem, s_send, s_recv, e_send, e_recv, c_send, c_recv, t_send, t_recv, d_send, d_recv,
):
    gx = lax.axis_index("gx")
    gy = lax.axis_index("gy")
    xl, xh = lax.rem(gx + nx - 1, nx), lax.rem(gx + 1, nx)
    yl, yh = lax.rem(gy + ny - 1, ny), lax.rem(gy + 1, ny)
    near = ((xl, gy), (xh, gy), (gx, yl), (gx, yh))
    corner = ((xl, yl), (xl, yh), (xh, yl), (xh, yh))
    has = (gx > 0, gx < nx - 1, gy > 0, gy < ny - 1)
    has_corner = (has[0] & has[2], has[0] & has[3], has[1] & has[2], has[1] & has[3])

    barrier = pltpu.get_barrier_semaphore()
    for s in (2, 3, 0, 1):

        @pl.when(has[s])
        def _():
            pl.semaphore_signal(barrier, inc=1, device_id=near[s], device_id_type=MESH)

    loads = [
        pltpu.make_async_copy(sol_ref, st, load_sem.at[0]),
        pltpu.make_async_copy(ins_ref, ins, load_sem.at[1]),
        pltpu.make_async_copy(imp_ref, imp, load_sem.at[2]),
        pltpu.make_async_copy(con_ref, con, load_sem.at[3]),
        pltpu.make_async_copy(war_ref, war, load_sem.at[4]),
        pltpu.make_async_copy(ele_ref, ele, load_sem.at[5]),
    ]
    for copy in loads:
        copy.start()

    lane = lax.broadcasted_iota(jnp.int32, (1, LANES), 1)
    lane4 = lane & 3
    tile_shape = (SIDE, LANES)
    last_lane = (lane != LANES - 1).astype(F32)
    last_row = (lax.broadcasted_iota(jnp.int32, (SIDE, LANES), 0) != SIDE - 1).astype(F32)

    def slab(x):
        return pl.ds(pl.multiple_of(x * SIDE, SIDE), SIDE)

    def remote(src, dst, send, recv, target):
        return pltpu.make_async_remote_copy(
            src_ref=src, dst_ref=dst, send_sem=send, recv_sem=recv, device_id=target, device_id_type=MESH
        )

    def start(copies, flags, order):
        for s in order:

            @pl.when(flags[s])
            def _():
                copies[s].start()

    def wait_sent(copies, flags):
        for s in range(4):

            @pl.when(flags[s])
            def _():
                copies[s].wait_send()

    def wait_arrived(copies, flags, opposite):
        for s in range(4):

            @pl.when(flags[s])
            def _():
                copies[opposite[s]].wait_recv()

    def state_copies(k):
        return [
            remote(sb.at[k, s], hb.at[k, OPPOSITE[s]], s_send.at[k, s], s_recv.at[k, OPPOSITE[s]], near[s])
            for s in range(4)
        ]

    def eps_copies():
        return [remote(se.at[s], hex_.at[OPPOSITE[s]], e_send.at[s], e_recv.at[OPPOSITE[s]], near[s]) for s in range(4)]

    def cond_copies():
        return [remote(cs, cr.at[OPPOSITE[s]], c_send.at[s], c_recv.at[OPPOSITE[s]], near[s]) for s in range(4)]

    def thermal_copies(t):
        sides, corners = [], []
        for s in range(4):
            o = OPPOSITE[s]
            sides.append(remote(ts.at[t], tr.at[t, o], t_send.at[t, s], t_recv.at[t, o], near[s]))
        for s in range(4):
            o = DIAGONAL_OPPOSITE[s]
            corners.append(remote(ds.at[t, s], dr.at[t, o], d_send.at[t, s], d_recv.at[t, o], corner[s]))
        return sides, corners

    def start_thermal(t):
        sides, corners = thermal_copies(t)
        start(sides, has, (2, 3))
        start(corners, has_corner, range(4))
        start(sides, has, (0, 1))

    def wait_thermal(t):
        sides, corners = thermal_copies(t)
        wait_arrived(sides, has, OPPOSITE)
        wait_arrived(corners, has_corner, DIAGONAL_OPPOSITE)

    def wait_thermal_sent(t):
        sides, corners = thermal_copies(t)
        wait_sent(sides, has)
        wait_sent(corners, has_corner)

    border = (
        pl.ds(0, SIDE), pl.ds(NODES - SIDE, SIDE), pl.ds(0, SIDE, stride=SIDE), pl.ds(SIDE - 1, SIDE, stride=SIDE)
    )

    def pack_thermal(t, warm, source):
        ts[t, 0:4, :] = warm
        ts[t, 4:8, :] = source
        tile = ts[t]
        up2, down2 = pltpu.roll(tile, 2, 1), pltpu.roll(tile, LANES - 2, 1)
        up3, down3 = pltpu.roll(tile, 3, 1), pltpu.roll(tile, LANES - 3, 1)

        def low(a, b):
            return jnp.where(lane4 < 2, tile[a:a + 1], jnp.where(lane4 == 2, up2[b:b + 1], up3[a + 4:a + 5]))

        def high(a, b):
            return jnp.where(lane4 >= 2, tile[a:a + 1], jnp.where(lane4 == 1, down2[b:b + 1], down3[a + 4:a + 5]))

        ds[t, 0, 0:1, :] = low(0, 1)
        ds[t, 1, 0:1, :] = high(0, 1)
        ds[t, 2, 0:1, :] = low(3, 2)
        ds[t, 3, 0:1, :] = high(3, 2)

    def keep(flag, a):
        return jnp.where(flag, a, jnp.zeros_like(a))

    def load_corners(t):
        for s in range(4):
            dd[s:s + 1, :] = keep(has_corner[s], dr[t, s, 0:1, :])

    def gather_source(t, into):
        tile = dd[...]
        up3, down3 = pltpu.roll(tile, 3, 1), pltpu.roll(tile, LANES - 3, 1)
        into[1, 0:2, :] = keep(has[0], tr[t, 0, 6:8, :])
        into[1, 2:6, :] = ts[t, 4:8, :]
        into[1, 6:8, :] = keep(has[1], tr[t, 1, 4:6, :])
        into[0, 2:6, :] = keep(has[2], tr[t, 2, 4:8, :])
        into[2, 2:6, :] = keep(has[3], tr[t, 3, 4:8, :])
        into[0, 1:2, :] = up3[0:1]
        into[0, 6:7, :] = up3[2:3]
        into[2, 1:2, :] = down3[1:2]
        into[2, 6:7, :] = down3[3:4]

    def gather_warm(t):
        tile = dd[...]
        up2, down2 = pltpu.roll(tile, 2, 1), pltpu.roll(tile, LANES - 2, 1)
        tx[1, 0:3, :] = keep(has[0], tr[t, 0, 1:4, :])
        tx[1, 3:7, :] = ts[t, 0:4, :]
        tx[1, 7:10, :] = keep(has[1], tr[t, 1, 0:3, :])
        tx[0, 3:7, :] = keep(has[2], tr[t, 2, 0:4, :])
        tx[2, 3:7, :] = keep(has[3], tr[t, 3, 0:4, :])
        tx[0, 1:2, :] = up2[0:1]
        tx[0, 2:3, :] = tile[0:1]
        tx[0, 7:8, :] = tile[2:3]
        tx[0, 8:9, :] = up2[2:3]
        tx[2, 1:2, :] = down2[1:2]
        tx[2, 2:3, :] = tile[1:2]
        tx[2, 7:8, :] = tile[3:4]
        tx[2, 8:9, :] = down2[3:4]

    def relax(t):
        load_corners(t)
        gather_source(t, sx)
        gather_warm(t)
        for _ in range(SWEEPS):
            mid = [tx[b, 1:9, :] for b in range(3)]
            new = []
            for b in range(3):
                c = mid[b]
                z_low = jnp.where(lane >= 4, pltpu.roll(c, 4, 1), 0.0)
                z_high = jnp.where(lane < LANES - 4, pltpu.roll(c, LANES - 4, 1), 0.0)
                y_low, y_high = pltpu.roll(c, 1, 1), pltpu.roll(c, LANES - 1, 1)
                if b > 0:
                    y_low = jnp.where(lane4 > 0, y_low, pltpu.roll(mid[b - 1], LANES - 3, 1))
                if b < 2:
                    y_high = jnp.where(lane4 < 3, y_high, pltpu.roll(mid[b + 1], 3, 1))
                total = (tx[b, 0:8, :] + tx[b, 2:10, :]) + (y_low + y_high) + (z_low + z_high)
                new.append((sx[b] + cx[b] * total) * ix[b])
            for b in range(3):
                tx[b, 1:9, :] = new[b]
        return tx[1, 3:7, :]

    for copy in loads:
        copy.wait()
    for s in range(4):
        for f in range(3):
            sb[0, s, f] = st[f, border[s], :]
    eps[...] = jnp.where(ins[...] == 1, 0.4, 1.0).astype(F32)
    for s in range(4):
        se[s] = eps[border[s], :]
        eleb[s] = ele[border[s], :]

    def lookup(labels, table):
        result = jnp.zeros(labels.shape, F32)
        for level, amount in enumerate(table):
            result = jnp.where(labels == level, amount, result)
        return result

    for c in range(CELLS):
        small[4 * c:4 * c + 4, :] = lookup(imp[c], (-2.0, -0.5, 0.5, 2.0))
        small[16 + 4 * c:16 + 4 * c + 4, :] = lookup(con[c], (0.5, 1.0, 2.0, 4.0))
        small[32 + 4 * c:32 + 4 * c + 4, :] = war[c]
    zc = LANES // 4
    wide = (lax.broadcasted_iota(jnp.int32, (zc, LANES), 1) // 4 == lax.broadcasted_iota(jnp.int32, (zc, LANES), 0)).astype(F32)
    rep[...] = jnp.dot(small[...], wide, precision=lax.Precision.HIGHEST, preferred_element_type=F32)
    for c in range(CELLS):
        for y in range(CELLS):
            row = jnp.broadcast_to(rep[4 * c + y:4 * c + y + 1, :], (4, LANES))
            dop[c, 4 * y:4 * y + 4, :] = row
            if c in (0, CELLS - 1):
                dopb[c // (CELLS - 1), 4 * y:4 * y + 4, :] = row
            if y in (0, CELLS - 1):
                dopb[2 + y // (CELLS - 1), 4 * c:4 * c + 4, :] = row

    def packed(first):
        rows = [rep[pl.ds(first + y, 4, stride=4), :] for y in range(CELLS)]
        return jnp.where(lane4 == 0, rows[0], jnp.where(lane4 == 1, rows[1], jnp.where(lane4 == 2, rows[2], rows[3])))

    cond, warm0 = packed(16), packed(32)
    cs[0:4, :] = cond
    cs[4:8, :] = cond
    ds[...] = jnp.zeros_like(ds)
    for s in range(4):
        at = (s // 2) * (CELLS - 1)
        ds[1, s, 1:2, :] = cs[at:at + 1, :]
    ts[1, 0:4, :] = warm0
    tx[...] = jnp.zeros_like(tx)
    sx[...] = jnp.zeros_like(sx)
    cx[...] = jnp.zeros_like(cx)
    dd[...] = jnp.zeros_like(dd)

    count = sum(flag.astype(jnp.int32) for flag in has)
    pl.semaphore_wait(barrier, count)
    start(state_copies(0), has, (2, 3, 0, 1))
    start(eps_copies(), has, (2, 3, 0, 1))
    start(cond_copies(), has, (2, 3, 0, 1))

    def weigh(x, below, upper):
        e = eps[slab(x), :]
        wy = (e + pltpu.roll(e, SIDE - 1, 0)) * last_row
        wz = (e + pltpu.roll(e, LANES - 1, 1)) * last_lane
        wl[1, slab(x), :] = wy
        wl[2, slab(x), :] = wz
        total = below + wy + pltpu.roll(wy, 1, 0) + wz + pltpu.roll(wz, 1, 1)
        if not upper:
            fc[slab(x), :] = total
            return below
        wx = e + eps[slab(x + 1), :]
        wl[0, slab(x), :] = wx
        fc[slab(x), :] = total + wx
        return wx

    zero = jnp.zeros((SIDE, LANES), F32)
    below = lax.fori_loop(0, SIDE - 1, lambda x, b: weigh(x, b, True), zero)
    weigh(SIDE - 1, below, False)

    def fluxes(x, below, upper):
        psi, n, p = (st[f, slab(x), :] for f in range(3))
        d, je, jh, gn, gp, g = face(psi, n, p, *(pltpu.roll(a, SIDE - 1, 0) for a in (psi, n, p)))
        je, jh, gn, gp, g, ld = (a * last_row for a in (je, jh, gn, gp, g, d))
        lap = wl[1, slab(x), :] * d
        t = je - jh
        sums = [je, jh, lap, ld, gn, gp, g, t * t]
        sums = [a - pltpu.roll(a, 1, 0) if i < 4 else a + pltpu.roll(a, 1, 0) for i, a in enumerate(sums)]
        d, je, jh, gn, gp, g = face(psi, n, p, *(pltpu.roll(a, LANES - 1, 1) for a in (psi, n, p)))
        je, jh, gn, gp, g, ld = (a * last_lane for a in (je, jh, gn, gp, g, d))
        lap = wl[2, slab(x), :] * d
        t = je - jh
        more = [je, jh, lap, ld, gn, gp, g, t * t]
        more = [a - pltpu.roll(a, 1, 1) if i < 4 else a + pltpu.roll(a, 1, 1) for i, a in enumerate(more)]
        sums = [a + b for a, b in zip(sums, more)]
        sums = [a - b if i < 4 else a + b for i, (a, b) in enumerate(zip(sums, below))]
        carry = below
        if upper:
            d, je, jh, gn, gp, g = face(psi, n, p, *(st[f, slab(x + 1), :] for f in range(3)))
            t = je - jh
            carry = (je, jh, wl[0, slab(x), :] * d, d, gn, gp, g, t * t)
            sums = [a + b for a, b in zip(sums, carry)]
        for q in range(7):
            acc[q, slab(x), :] = sums[q]
        cell = slab(x // CELLS)
        hs[cell, :] = hs[cell, :] + sums[7] / (n + p)
        return carry

    def newton(state, sums, faces, mu, level, contact):
        psi, n, p = state
        fe, fh, lap, ls, gn, gp, gs = sums
        rd = 1.0 / (n + p + 2.0)
        rec = (n * p - 1.0) * rd
        rn, rp = (p + 1.0) * rd, (n + 1.0) * rd
        rn, rp = rn * rn, rp * rp
        r0 = lap + CHARGE * (p - n + level)
        r1 = mu * fe - rec
        r2 = mu * fh - rec
        aa = -faces
        ba, ca = mu * gn, mu * gp
        bb = -mu * (gs + 0.5 * ls) - rn - SHIFT
        cc = -mu * (gs - 0.5 * ls) - rp - SHIFT
        bc, cb = -rp, -rn
        c_aa = bb * cc - bc * cb
        c_ab = bc * ca - ba * cc
        c_ac = ba * cb - bb * ca
        inv = 1.0 / (aa * c_aa + CHARGE * (c_ac - c_ab))
        d0 = (c_aa * r0 + CHARGE * ((cb + cc) * r1 - (bc + bb) * r2)) * inv
        d1 = (c_ab * r0 + (aa * cc - CHARGE * ca) * r1 + (CHARGE * ba - aa * bc) * r2) * inv
        d2 = (c_ac * r0 - (CHARGE * ca + aa * cb) * r1 + (aa * bb + CHARGE * ba) * r2) * inv
        d0 = jnp.where(contact, psi - BIAS * level, d0)
        d1 = jnp.where(contact, n - 1.0, d1)
        d2 = jnp.where(contact, p - 1.0, d2)
        return psi - d0, n * jnp.exp(-d1 / n), p * jnp.exp(-d2 / p)

    def pick(rows):
        return jnp.where(lane4 == 0, rows[0], jnp.where(lane4 == 1, rows[1], jnp.where(lane4 == 2, rows[2], rows[3])))

    def stack(ref, *index):
        return jnp.concatenate([ref[index[:1] + (s,) + index[1:]] if len(index) > 1 else ref[s] for s in range(4)], 0)

    def step(k, nothing):
        following = jnp.minimum(k + 1, NEWTON - 1)

        hs[...] = jnp.zeros_like(hs)
        none = (zero,) * 8
        below = lax.fori_loop(0, SIDE - 1, lambda x, b: fluxes(x, b, True), none)
        fluxes(SIDE - 1, below, False)
        parts = []
        for y in range(CELLS):
            total = hs[pl.ds(4 * y, 4, stride=SIDE), :]
            for i in range(1, 4):
                total = total + hs[pl.ds(4 * y + i, 4, stride=SIDE), :]
            parts.append(total)
        rep[0:16, :] = spread(jnp.concatenate(parts, 0), lane)
        hin[0:4, :] = pick([rep[4 * y:4 * y + 4, :] for y in range(CELLS)])

        @pl.when(k == 1)
        def _():
            wait_thermal(1)
            for s, (b, r) in enumerate(((0, 1), (2, 1), (0, 6), (2, 6))):
                cx[b, r:r + 1, :] = keep(has_corner[s], dr[1, s, 1:2, :])
            ix[...] = 1.0 / (SINK + 6.0 * cx[...])

        @pl.when(k > 1)
        def _():
            wait_thermal(k)

        @pl.when(k > 0)
        def _():
            ts[k + 1, 0:4, :] = relax(k)

        warm = ts[k + 1, 0:4, :]
        m = 1.0 / (1.0 + DROP * warm)

        wait_arrived(state_copies(k), has, OPPOSITE)
        mine = [stack(sb, k, f) for f in range(3)]
        scale = jnp.concatenate([jnp.broadcast_to(flag.astype(F32), tile_shape) for flag in has], 0)
        halo = [jnp.where(scale > 0.0, stack(hb, k, f), own) for f, own in enumerate(mine)]
        d, je, jh, gn, gp, g = face(*mine, *halo)
        t = (je - jh) * scale
        qe[...] = t * t / (mine[1] + mine[2])
        edge = qe[pl.ds(0, 16, stride=4), :]
        for i in range(1, 4):
            edge = edge + qe[pl.ds(i, 16, stride=4), :]
        rep[0:16, :] = spread(edge, lane)
        heat = hin[0:4, :] + jnp.where(lane4 == 0, rep[8:12, :], jnp.where(lane4 == 3, rep[12:16, :], 0.0))
        hin[0:4, :] = heat
        for c in range(2):
            at = c * (CELLS - 1)
            hin[at:at + 1, :] = hin[at:at + 1, :] + pick([rep[4 * c + y:4 * c + y + 1, :] for y in range(CELLS)])
        pack_thermal(k + 1, warm, hin[0:4, :] * m * (HEAT_GAIN * 0.5 / 64.0))
        start_thermal(k + 1)

        @pl.when(k == 0)
        def _():
            wait_arrived(eps_copies(), has, OPPOSITE)
            for s in range(4):
                wb[s] = keep(has[s], se[s] + hex_[s])
                fc[border[s], :] = fc[border[s], :] + wb[s]
            for s in range(4):
                fcb[s] = fc[border[s], :]

        sums = (je * scale, jh * scale, stack(wb) * d, d * scale, gn * scale, gp * scale, g * scale)
        for s in range(4):
            for q in range(7):
                acc[q, border[s], :] = acc[q, border[s], :] + sums[q][SIDE * s:SIDE * s + SIDE]
        m4 = spread(jnp.concatenate([jnp.where(lane4 == y, m, 0.0) for y in range(CELLS)], 0), lane)
        rep[0:16, :] = m4
        for a in range(2):
            at = a * (CELLS - 1)
            for b in range(CELLS):
                mobb[a, 4 * b:4 * b + 4, :] = jnp.broadcast_to(rep[4 * b + at:4 * b + at + 1, :], (4, LANES))
                mobb[2 + a, 4 * b:4 * b + 4, :] = jnp.broadcast_to(rep[4 * at + b:4 * at + b + 1, :], (4, LANES))

        @pl.when(k < NEWTON - 1)
        def _():
            for pair in ((2, 3), (0, 1)):
                new = []
                for s in pair:
                    new.append(newton(
                        [sb[k, s, f] for f in range(3)], [acc[q, border[s], :] for q in range(7)],
                        fcb[s], mobb[s], dopb[s], eleb[s] == 1,
                    ))
                for s, values in zip(pair, new):
                    for f in range(3):
                        sb[following, s, f] = values[f]
                start(state_copies(following), has, pair)

        for c in range(CELLS):
            for y in range(CELLS):
                mob[c, 4 * y:4 * y + 4, :] = jnp.broadcast_to(rep[4 * y + c:4 * y + c + 1, :], (4, LANES))

        @pl.when(k == 0)
        def _():
            wait_sent(eps_copies(), has)
            wait_sent(cond_copies(), has)
            wait_arrived(cond_copies(), has, OPPOSITE)
            cx[1, 0:2, :] = keep(has[0], cr[0, 2:4, :])
            cx[1, 2:6, :] = cs[0:4, :]
            cx[1, 6:8, :] = keep(has[1], cr[1, 0:2, :])
            cx[0, 2:6, :] = keep(has[2], cr[2, 0:4, :])
            cx[2, 2:6, :] = keep(has[3], cr[3, 0:4, :])

        def solve(x, nothing):
            rows = slab(x)
            cell = x // CELLS
            new = newton(
                [st[f, rows, :] for f in range(3)], [acc[q, rows, :] for q in range(7)],
                fc[rows, :], mob[cell], dop[cell], ele[rows, :] == 1,
            )
            for f in range(3):
                st[f, rows, :] = new[f]
            return nothing

        lax.fori_loop(0, SIDE, solve, 0)
        wait_sent(state_copies(k), has)

        @pl.when(k > 0)
        def _():
            wait_thermal_sent(k)

        return nothing

    lax.fori_loop(0, NEWTON, step, 0)

    wait_thermal(NEWTON)
    temp_ref[0:4, :] = relax(NEWTON)
    wait_thermal_sent(NEWTON)


def emit(st_ref, warm_ref, out_ref, temp_out, temp_ref, sem):
    store = pltpu.make_async_copy(st_ref, out_ref, sem.at[0])
    store.start()
    warm = warm_ref[0:4, :]
    lane4 = lax.broadcasted_iota(jnp.int32, (1, LANES), 1) & 3
    zc = LANES // 4
    cells = jnp.concatenate([jnp.where(lane4 == y, warm, 0.0) for y in range(CELLS)], 0)
    narrow = (lax.broadcasted_iota(jnp.int32, (LANES, zc), 0) // 4 == lax.broadcasted_iota(jnp.int32, (LANES, zc), 1)).astype(F32)
    cells = jnp.dot(cells, narrow, precision=lax.Precision.HIGHEST, preferred_element_type=F32)
    for c in range(CELLS):
        for y in range(CELLS):
            temp_ref[c, y:y + 1, :] = cells[4 * y + c:4 * y + c + 1, :]
    last = pltpu.make_async_copy(temp_ref, temp_out, sem.at[1])
    last.start()
    store.wait()
    last.wait()


def solution(mesh):
    nx, ny = mesh.shape["gx"], mesh.shape["gy"]

    def per_device(sol, ins, ele, imp, con, war):
        vm = pltpu.VMEM
        dma = pltpu.SemaphoreType.DMA
        tile = (SIDE, LANES)
        call = pl.pallas_call(
            functools.partial(body, nx, ny),
            out_shape=(
                pltpu.VMEM((3, NODES, LANES), F32),
                pltpu.VMEM((8, LANES), F32),
            ),
            in_specs=[pl.BlockSpec(memory_space=pl.ANY)] * 6,
            out_specs=(pl.BlockSpec(memory_space=pltpu.VMEM), pl.BlockSpec(memory_space=pltpu.VMEM)),
            scratch_shapes=[
                vm((NODES, LANES), F32),
                vm((NODES, LANES), jnp.int32),
                vm((NODES, LANES), jnp.int32),
                vm((CELLS, CELLS, LANES // 4), jnp.int32),
                vm((CELLS, CELLS, LANES // 4), jnp.int32),
                vm((CELLS, CELLS, LANES // 4), F32),
                vm((3, NODES, LANES), F32),
                vm((NODES, LANES), F32),
                vm((7, NODES, LANES), F32),
                vm((64, LANES), F32),
                vm((64, LANES), F32),
                vm((8, LANES), F32),
                vm((CELLS,) + tile, F32),
                vm((CELLS,) + tile, F32),
                vm((4,) + tile, F32),
                vm((4,) + tile, F32),
                vm((4,) + tile, F32),
                vm((4,) + tile, jnp.int32),
                vm((48, LANES), F32),
                vm((48, LANES // 4), F32),
                vm((4,) + tile, F32),
                vm((NEWTON, 4, 3) + tile, F32),
                vm((4,) + tile, F32),
                vm((4,) + tile, F32),
                vm((NEWTON, 4, 3) + tile, F32),
                vm((8, LANES), F32),
                vm((4, 8, LANES), F32),
                vm((NEWTON + 1, 8, LANES), F32),
                vm((NEWTON + 1, 4, 2, LANES), F32),
                vm((NEWTON + 1, 4, 8, LANES), F32),
                vm((NEWTON + 1, 4, 2, LANES), F32),
                vm((3, SIDE, LANES), F32),
                vm((3, 8, LANES), F32),
                vm((3, 8, LANES), F32),
                vm((3, 8, LANES), F32),
                vm((8, LANES), F32),
                dma((6,)),
                dma((NEWTON, 4)),
                dma((NEWTON, 4)),
                dma((4,)),
                dma((4,)),
                dma((4,)),
                dma((4,)),
                dma((NEWTON + 1, 4)),
                dma((NEWTON + 1, 4)),
                dma((NEWTON + 1, 4)),
                dma((NEWTON + 1, 4)),
            ],
            compiler_params=pltpu.CompilerParams(collective_id=0, has_side_effects=True),
        )
        state, warm = call(
            sol.reshape(3, NODES, LANES), ins.reshape(NODES, LANES), ele.reshape(NODES, LANES), imp, con, war
        )
        state = pltpu.with_memory_space_constraint(state, pltpu.VMEM)
        warm = pltpu.with_memory_space_constraint(warm, pltpu.VMEM)
        state, warm = pl.pallas_call(
            emit,
            out_shape=(
                jax.ShapeDtypeStruct((3, NODES, LANES), F32),
                jax.ShapeDtypeStruct((CELLS, CELLS, LANES // 4), F32),
            ),
            in_specs=[pl.BlockSpec(memory_space=pltpu.VMEM), pl.BlockSpec(memory_space=pltpu.VMEM)],
            out_specs=(pl.BlockSpec(memory_space=pl.ANY), pl.BlockSpec(memory_space=pl.ANY)),
            scratch_shapes=[vm((CELLS, CELLS, LANES // 4), F32), dma((2,))],
        )(state, warm)
        return state.reshape(3, SIDE, SIDE, LANES), warm

    spec = P("gx", "gy", None)
    return jax.shard_map(
        per_device,
        mesh=mesh,
        in_specs=(P(None, "gx", "gy", None),) + (spec,) * 5,
        out_specs=(P(None, "gx", "gy", None), spec),
        check_vma=False,
    )
```

```python
import functools

import jax
import jax.numpy as jnp
from jax import lax
from jax.experimental import pallas as pl
from jax.experimental.pallas import tpu as pltpu
from jax.sharding import PartitionSpec as P

NEWTON = 3
SWEEPS = 3
SIDE = 16
LANES = 128
CELLS = 4
NODES = SIDE * SIDE

CHARGE = 4.0
SHIFT = 24.0
BIAS = 0.25
HEAT_GAIN = 1.0
SINK = 0.3
DROP = 0.5

STATE_ROWS = 3 * SIDE
EPS_AT = STATE_ROWS
COND_AT = EPS_AT + SIDE
FIRST_ROWS = COND_AT + 8

F32 = jnp.float32
MESH = pl.DeviceIdType.MESH
OPPOSITE = (1, 0, 3, 2)
DIAGONAL_OPPOSITE = (3, 2, 1, 0)


def face(pi, ni, qi, pj, nj, qj):
    d = pj - pi
    u = jnp.abs(d)
    v = d * d
    small = u < 0.5
    r = 1.0 / (jnp.exp(u) - 1.0)
    wide = u * r
    g_near = 1.0 + v * (1.0 / 12.0 + v * (-1.0 / 720.0 + v * (1.0 / 30240.0 + v * (-1.0 / 1209600.0))))
    h_near = u * (1.0 / 6.0 + v * (-1.0 / 180.0 + v * (1.0 / 5040.0 + v * (-1.0 / 151200.0))))
    b = jnp.where(small, g_near - 0.5 * u, wide)
    h = jnp.where(small, h_near, r * (1.0 - wide) - wide + 0.5)
    g = b + 0.5 * u
    h = jnp.where(d < 0.0, -h, h)
    plus = b + jnp.maximum(-d, 0.0)
    minus = b + jnp.maximum(d, 0.0)
    je = nj * plus - ni * minus
    jh = qj * minus - qi * plus
    gn = 0.5 * (nj + ni) - h * (nj - ni)
    gp = -0.5 * (qj + qi) - h * (qj - qi)
    return d, je, jh, gn, gp, g


def spread(a, lane):
    a = a + jnp.where((lane & 1) == 0, pltpu.roll(a, LANES - 1, 1), pltpu.roll(a, 1, 1))
    return a + jnp.where((lane & 2) == 0, pltpu.roll(a, LANES - 2, 1), pltpu.roll(a, 2, 1))


def body(
    nx, ny,
    sol_ref, ins_ref, ele_ref, imp_ref, con_ref, war_ref,
    st, temp_ref,
    eps, ins, ele, imp, con, war, wl, fc, acc, hs, qe, hin, mob, dop, mobb, dopb, fcb, eleb, rep, small, wb,
    hb, sb, ts, ds, tr, dr, tx, sx, cx, ix, dd,
    load_sem, s_send, s_recv, t_send, t_recv, d_send, d_recv,
):
    gx = lax.axis_index("gx")
    gy = lax.axis_index("gy")
    xl, xh = lax.rem(gx + nx - 1, nx), lax.rem(gx + 1, nx)
    yl, yh = lax.rem(gy + ny - 1, ny), lax.rem(gy + 1, ny)
    near = ((xl, gy), (xh, gy), (gx, yl), (gx, yh))
    corner = ((xl, yl), (xl, yh), (xh, yl), (xh, yh))
    has = (gx > 0, gx < nx - 1, gy > 0, gy < ny - 1)
    has_corner = (has[0] & has[2], has[0] & has[3], has[1] & has[2], has[1] & has[3])

    barrier = pltpu.get_barrier_semaphore()
    for s in (2, 3, 0, 1):

        @pl.when(has[s])
        def _():
            pl.semaphore_signal(barrier, inc=1, device_id=near[s], device_id_type=MESH)

    loads = [
        pltpu.make_async_copy(sol_ref, st, load_sem.at[0]),
        pltpu.make_async_copy(ins_ref, ins, load_sem.at[1]),
        pltpu.make_async_copy(imp_ref, imp, load_sem.at[2]),
        pltpu.make_async_copy(con_ref, con, load_sem.at[3]),
        pltpu.make_async_copy(war_ref, war, load_sem.at[4]),
        pltpu.make_async_copy(ele_ref, ele, load_sem.at[5]),
    ]
    for copy in loads:
        copy.start()

    lane = lax.broadcasted_iota(jnp.int32, (1, LANES), 1)
    lane4 = lane & 3
    tile_shape = (SIDE, LANES)
    last_lane = (lane != LANES - 1).astype(F32)
    last_row = (lax.broadcasted_iota(jnp.int32, (SIDE, LANES), 0) != SIDE - 1).astype(F32)

    def slab(x):
        return pl.ds(pl.multiple_of(x * SIDE, SIDE), SIDE)

    def remote(src, dst, send, recv, target):
        return pltpu.make_async_remote_copy(
            src_ref=src, dst_ref=dst, send_sem=send, recv_sem=recv, device_id=target, device_id_type=MESH
        )

    def start(copies, flags, order):
        for s in order:

            @pl.when(flags[s])
            def _():
                copies[s].start()

    def start_state(copies, pair):
        if pair == (2, 3):
            start(copies, has, pair)
            return
        even = lax.rem(gx, 2) == 0
        start(copies, (has[0] & even, has[1]), (0, 1))
        start(copies, (has[0] & jnp.logical_not(even),), (0,))

    def wait_sent(copies, flags):
        for s in range(4):

            @pl.when(flags[s])
            def _():
                copies[s].wait_send()

    def wait_arrived(copies, flags, opposite):
        for s in range(4):

            @pl.when(flags[s])
            def _():
                copies[opposite[s]].wait_recv()

    def state_copies(k, rows=STATE_ROWS):
        return [
            remote(
                sb.at[k, s, pl.ds(0, rows), :], hb.at[k, OPPOSITE[s], pl.ds(0, rows), :],
                s_send.at[k, s], s_recv.at[k, OPPOSITE[s]], near[s],
            )
            for s in range(4)
        ]

    def first_copies():
        return state_copies(0, FIRST_ROWS)

    def thermal_copies(t):
        sides, corners = [], []
        for s in range(4):
            o = OPPOSITE[s]
            sides.append(remote(ts.at[t], tr.at[t, o], t_send.at[t, s], t_recv.at[t, o], near[s]))
        for s in range(4):
            o = DIAGONAL_OPPOSITE[s]
            corners.append(remote(ds.at[t, s], dr.at[t, o], d_send.at[t, s], d_recv.at[t, o], corner[s]))
        return sides, corners

    def start_thermal(t):
        sides, corners = thermal_copies(t)
        start(corners, has_corner, range(4))
        start(sides, has, (2, 3, 0, 1))

    def wait_thermal(t):
        sides, corners = thermal_copies(t)
        wait_arrived(sides, has, OPPOSITE)
        wait_arrived(corners, has_corner, DIAGONAL_OPPOSITE)

    def wait_thermal_sent(t):
        sides, corners = thermal_copies(t)
        wait_sent(sides, has)
        wait_sent(corners, has_corner)

    border = (
        pl.ds(0, SIDE), pl.ds(NODES - SIDE, SIDE), pl.ds(0, SIDE, stride=SIDE), pl.ds(SIDE - 1, SIDE, stride=SIDE)
    )

    def pack_thermal(t, warm, source):
        ts[t, 0:4, :] = warm
        ts[t, 4:8, :] = source
        tile = ts[t]
        up2, down2 = pltpu.roll(tile, 2, 1), pltpu.roll(tile, LANES - 2, 1)
        up3, down3 = pltpu.roll(tile, 3, 1), pltpu.roll(tile, LANES - 3, 1)

        def low(a, b):
            return jnp.where(lane4 < 2, tile[a:a + 1], jnp.where(lane4 == 2, up2[b:b + 1], up3[a + 4:a + 5]))

        def high(a, b):
            return jnp.where(lane4 >= 2, tile[a:a + 1], jnp.where(lane4 == 1, down2[b:b + 1], down3[a + 4:a + 5]))

        ds[t, 0, 0:1, :] = low(0, 1)
        ds[t, 1, 0:1, :] = high(0, 1)
        ds[t, 2, 0:1, :] = low(3, 2)
        ds[t, 3, 0:1, :] = high(3, 2)

    def keep(flag, a):
        return jnp.where(flag, a, jnp.zeros_like(a))

    def load_corners(t):
        for s in range(4):
            dd[s:s + 1, :] = keep(has_corner[s], dr[t, s, 0:1, :])

    def gather_source(t, into):
        tile = dd[...]
        up3, down3 = pltpu.roll(tile, 3, 1), pltpu.roll(tile, LANES - 3, 1)
        into[1, 0:2, :] = keep(has[0], tr[t, 0, 6:8, :])
        into[1, 2:6, :] = ts[t, 4:8, :]
        into[1, 6:8, :] = keep(has[1], tr[t, 1, 4:6, :])
        into[0, 2:6, :] = keep(has[2], tr[t, 2, 4:8, :])
        into[2, 2:6, :] = keep(has[3], tr[t, 3, 4:8, :])
        into[0, 1:2, :] = up3[0:1]
        into[0, 6:7, :] = up3[2:3]
        into[2, 1:2, :] = down3[1:2]
        into[2, 6:7, :] = down3[3:4]

    def gather_warm(t):
        tile = dd[...]
        up2, down2 = pltpu.roll(tile, 2, 1), pltpu.roll(tile, LANES - 2, 1)
        tx[1, 0:3, :] = keep(has[0], tr[t, 0, 1:4, :])
        tx[1, 3:7, :] = ts[t, 0:4, :]
        tx[1, 7:10, :] = keep(has[1], tr[t, 1, 0:3, :])
        tx[0, 3:7, :] = keep(has[2], tr[t, 2, 0:4, :])
        tx[2, 3:7, :] = keep(has[3], tr[t, 3, 0:4, :])
        tx[0, 1:2, :] = up2[0:1]
        tx[0, 2:3, :] = tile[0:1]
        tx[0, 7:8, :] = tile[2:3]
        tx[0, 8:9, :] = up2[2:3]
        tx[2, 1:2, :] = down2[1:2]
        tx[2, 2:3, :] = tile[1:2]
        tx[2, 7:8, :] = tile[3:4]
        tx[2, 8:9, :] = down2[3:4]

    def relax(t):
        load_corners(t)
        gather_source(t, sx)
        gather_warm(t)
        for _ in range(SWEEPS):
            mid = [tx[b, 1:9, :] for b in range(3)]
            new = []
            for b in range(3):
                c = mid[b]
                z_low = jnp.where(lane >= 4, pltpu.roll(c, 4, 1), 0.0)
                z_high = jnp.where(lane < LANES - 4, pltpu.roll(c, LANES - 4, 1), 0.0)
                y_low, y_high = pltpu.roll(c, 1, 1), pltpu.roll(c, LANES - 1, 1)
                if b > 0:
                    y_low = jnp.where(lane4 > 0, y_low, pltpu.roll(mid[b - 1], LANES - 3, 1))
                if b < 2:
                    y_high = jnp.where(lane4 < 3, y_high, pltpu.roll(mid[b + 1], 3, 1))
                total = (tx[b, 0:8, :] + tx[b, 2:10, :]) + (y_low + y_high) + (z_low + z_high)
                new.append((sx[b] + cx[b] * total) * ix[b])
            for b in range(3):
                tx[b, 1:9, :] = new[b]
        return tx[1, 3:7, :]

    for copy in loads:
        copy.wait()
    for s in range(4):
        for f in range(3):
            sb[0, s, SIDE * f:SIDE * f + SIDE, :] = st[f, border[s], :]
    eps[...] = jnp.where(ins[...] == 1, 0.4, 1.0).astype(F32)
    for s in range(4):
        sb[0, s, EPS_AT:EPS_AT + SIDE, :] = eps[border[s], :]
        eleb[s] = ele[border[s], :]

    def lookup(labels, table):
        result = jnp.zeros(labels.shape, F32)
        for level, amount in enumerate(table):
            result = jnp.where(labels == level, amount, result)
        return result

    for c in range(CELLS):
        small[4 * c:4 * c + 4, :] = lookup(imp[c], (-2.0, -0.5, 0.5, 2.0))
        small[16 + 4 * c:16 + 4 * c + 4, :] = lookup(con[c], (0.5, 1.0, 2.0, 4.0))
        small[32 + 4 * c:32 + 4 * c + 4, :] = war[c]
    zc = LANES // 4
    wide = (lax.broadcasted_iota(jnp.int32, (zc, LANES), 1) // 4 == lax.broadcasted_iota(jnp.int32, (zc, LANES), 0)).astype(F32)
    rep[...] = jnp.dot(small[...], wide, precision=lax.Precision.HIGHEST, preferred_element_type=F32)
    for c in range(CELLS):
        for y in range(CELLS):
            row = jnp.broadcast_to(rep[4 * c + y:4 * c + y + 1, :], (4, LANES))
            dop[c, 4 * y:4 * y + 4, :] = row
            if c in (0, CELLS - 1):
                dopb[c // (CELLS - 1), 4 * y:4 * y + 4, :] = row
            if y in (0, CELLS - 1):
                dopb[2 + y // (CELLS - 1), 4 * c:4 * c + 4, :] = row

    def packed(first):
        rows = [rep[pl.ds(first + y, 4, stride=4), :] for y in range(CELLS)]
        return jnp.where(lane4 == 0, rows[0], jnp.where(lane4 == 1, rows[1], jnp.where(lane4 == 2, rows[2], rows[3])))

    cond, warm0 = packed(16), packed(32)
    for s in range(4):
        sb[0, s, COND_AT:COND_AT + 4, :] = cond
        sb[0, s, COND_AT + 4:COND_AT + 8, :] = cond
    ds[...] = jnp.zeros_like(ds)
    for s in range(4):
        at = (s // 2) * (CELLS - 1)
        ds[1, s, 1:2, :] = sb[0, 0, COND_AT + at:COND_AT + at + 1, :]
    ts[1, 0:4, :] = warm0
    tx[...] = jnp.zeros_like(tx)
    sx[...] = jnp.zeros_like(sx)
    cx[...] = jnp.zeros_like(cx)
    dd[...] = jnp.zeros_like(dd)

    count = sum(flag.astype(jnp.int32) for flag in has)
    pl.semaphore_wait(barrier, count)
    start_state(first_copies(), (2, 3))
    start_state(first_copies(), (0, 1))

    def weigh(x, below, upper):
        e = eps[slab(x), :]
        wy = (e + pltpu.roll(e, SIDE - 1, 0)) * last_row
        wz = (e + pltpu.roll(e, LANES - 1, 1)) * last_lane
        wl[1, slab(x), :] = wy
        wl[2, slab(x), :] = wz
        total = below + wy + pltpu.roll(wy, 1, 0) + wz + pltpu.roll(wz, 1, 1)
        if not upper:
            fc[slab(x), :] = total
            return below
        wx = e + eps[slab(x + 1), :]
        wl[0, slab(x), :] = wx
        fc[slab(x), :] = total + wx
        return wx

    zero = jnp.zeros((SIDE, LANES), F32)
    below = lax.fori_loop(0, SIDE - 1, lambda x, b: weigh(x, b, True), zero)
    weigh(SIDE - 1, below, False)

    def fluxes(x, below, upper):
        psi, n, p = (st[f, slab(x), :] for f in range(3))
        d, je, jh, gn, gp, g = face(psi, n, p, *(pltpu.roll(a, SIDE - 1, 0) for a in (psi, n, p)))
        je, jh, gn, gp, g, ld = (a * last_row for a in (je, jh, gn, gp, g, d))
        lap = wl[1, slab(x), :] * d
        t = je - jh
        sums = [je, jh, lap, ld, gn, gp, g, t * t]
        sums = [a - pltpu.roll(a, 1, 0) if i < 4 else a + pltpu.roll(a, 1, 0) for i, a in enumerate(sums)]
        d, je, jh, gn, gp, g = face(psi, n, p, *(pltpu.roll(a, LANES - 1, 1) for a in (psi, n, p)))
        je, jh, gn, gp, g, ld = (a * last_lane for a in (je, jh, gn, gp, g, d))
        lap = wl[2, slab(x), :] * d
        t = je - jh
        more = [je, jh, lap, ld, gn, gp, g, t * t]
        more = [a - pltpu.roll(a, 1, 1) if i < 4 else a + pltpu.roll(a, 1, 1) for i, a in enumerate(more)]
        sums = [a + b for a, b in zip(sums, more)]
        sums = [a - b if i < 4 else a + b for i, (a, b) in enumerate(zip(sums, below))]
        carry = below
        if upper:
            d, je, jh, gn, gp, g = face(psi, n, p, *(st[f, slab(x + 1), :] for f in range(3)))
            t = je - jh
            carry = (je, jh, wl[0, slab(x), :] * d, d, gn, gp, g, t * t)
            sums = [a + b for a, b in zip(sums, carry)]
        for q in range(7):
            acc[q, slab(x), :] = sums[q]
        cell = slab(x // CELLS)
        hs[cell, :] = hs[cell, :] + sums[7] / (n + p)
        return carry

    def newton(state, sums, faces, mu, level, contact):
        psi, n, p = state
        fe, fh, lap, ls, gn, gp, gs = sums
        rd = 1.0 / (n + p + 2.0)
        rec = (n * p - 1.0) * rd
        rn, rp = (p + 1.0) * rd, (n + 1.0) * rd
        rn, rp = rn * rn, rp * rp
        r0 = lap + CHARGE * (p - n + level)
        r1 = mu * fe - rec
        r2 = mu * fh - rec
        aa = -faces
        ba, ca = mu * gn, mu * gp
        bb = -mu * (gs + 0.5 * ls) - rn - SHIFT
        cc = -mu * (gs - 0.5 * ls) - rp - SHIFT
        bc, cb = -rp, -rn
        c_aa = bb * cc - bc * cb
        c_ab = bc * ca - ba * cc
        c_ac = ba * cb - bb * ca
        inv = 1.0 / (aa * c_aa + CHARGE * (c_ac - c_ab))
        d0 = (c_aa * r0 + CHARGE * ((cb + cc) * r1 - (bc + bb) * r2)) * inv
        d1 = (c_ab * r0 + (aa * cc - CHARGE * ca) * r1 + (CHARGE * ba - aa * bc) * r2) * inv
        d2 = (c_ac * r0 - (CHARGE * ca + aa * cb) * r1 + (aa * bb + CHARGE * ba) * r2) * inv
        d0 = jnp.where(contact, psi - BIAS * level, d0)
        d1 = jnp.where(contact, n - 1.0, d1)
        d2 = jnp.where(contact, p - 1.0, d2)
        return psi - d0, n * jnp.exp(-d1 / n), p * jnp.exp(-d2 / p)

    def pick(rows):
        return jnp.where(lane4 == 0, rows[0], jnp.where(lane4 == 1, rows[1], jnp.where(lane4 == 2, rows[2], rows[3])))

    def stack(ref, *index):
        if not index:
            return jnp.concatenate([ref[s] for s in range(4)], 0)
        k, f = index
        return jnp.concatenate([ref[k, s, SIDE * f:SIDE * f + SIDE, :] for s in range(4)], 0)

    def step(k, nothing):
        following = jnp.minimum(k + 1, NEWTON - 1)

        hs[...] = jnp.zeros_like(hs)
        none = (zero,) * 8
        below = lax.fori_loop(0, SIDE - 1, lambda x, b: fluxes(x, b, True), none)
        fluxes(SIDE - 1, below, False)
        parts = []
        for y in range(CELLS):
            total = hs[pl.ds(4 * y, 4, stride=SIDE), :]
            for i in range(1, 4):
                total = total + hs[pl.ds(4 * y + i, 4, stride=SIDE), :]
            parts.append(total)
        rep[0:16, :] = spread(jnp.concatenate(parts, 0), lane)
        hin[0:4, :] = pick([rep[4 * y:4 * y + 4, :] for y in range(CELLS)])

        @pl.when(k == 1)
        def _():
            wait_thermal(1)
            for s, (b, r) in enumerate(((0, 1), (2, 1), (0, 6), (2, 6))):
                cx[b, r:r + 1, :] = keep(has_corner[s], dr[1, s, 1:2, :])
            ix[...] = 1.0 / (SINK + 6.0 * cx[...])

        @pl.when(k > 1)
        def _():
            wait_thermal(k)

        @pl.when(k > 0)
        def _():
            ts[k + 1, 0:4, :] = relax(k)

        warm = ts[k + 1, 0:4, :]
        m = 1.0 / (1.0 + DROP * warm)

        @pl.when(k == 0)
        def _():
            wait_arrived(first_copies(), has, OPPOSITE)

        @pl.when(k > 0)
        def _():
            wait_arrived(state_copies(k), has, OPPOSITE)

        mine = [stack(sb, k, f) for f in range(3)]
        scale = jnp.concatenate([jnp.broadcast_to(flag.astype(F32), tile_shape) for flag in has], 0)
        halo = [jnp.where(scale > 0.0, stack(hb, k, f), own) for f, own in enumerate(mine)]
        d, je, jh, gn, gp, g = face(*mine, *halo)
        t = (je - jh) * scale
        qe[...] = t * t / (mine[1] + mine[2])
        edge = qe[pl.ds(0, 16, stride=4), :]
        for i in range(1, 4):
            edge = edge + qe[pl.ds(i, 16, stride=4), :]
        rep[0:16, :] = spread(edge, lane)
        heat = hin[0:4, :] + jnp.where(lane4 == 0, rep[8:12, :], jnp.where(lane4 == 3, rep[12:16, :], 0.0))
        hin[0:4, :] = heat
        for c in range(2):
            at = c * (CELLS - 1)
            hin[at:at + 1, :] = hin[at:at + 1, :] + pick([rep[4 * c + y:4 * c + y + 1, :] for y in range(CELLS)])
        pack_thermal(k + 1, warm, hin[0:4, :] * m * (HEAT_GAIN * 0.5 / 64.0))
        start_thermal(k + 1)

        @pl.when(k == 0)
        def _():
            for s in range(4):
                wb[s] = keep(has[s], sb[0, s, EPS_AT:EPS_AT + SIDE, :] + hb[0, s, EPS_AT:EPS_AT + SIDE, :])
                fc[border[s], :] = fc[border[s], :] + wb[s]
            for s in range(4):
                fcb[s] = fc[border[s], :]

        sums = (je * scale, jh * scale, stack(wb) * d, d * scale, gn * scale, gp * scale, g * scale)
        for s in range(4):
            for q in range(7):
                acc[q, border[s], :] = acc[q, border[s], :] + sums[q][SIDE * s:SIDE * s + SIDE]
        m4 = spread(jnp.concatenate([jnp.where(lane4 == y, m, 0.0) for y in range(CELLS)], 0), lane)
        rep[0:16, :] = m4
        for a in range(2):
            at = a * (CELLS - 1)
            for b in range(CELLS):
                mobb[a, 4 * b:4 * b + 4, :] = jnp.broadcast_to(rep[4 * b + at:4 * b + at + 1, :], (4, LANES))
                mobb[2 + a, 4 * b:4 * b + 4, :] = jnp.broadcast_to(rep[4 * at + b:4 * at + b + 1, :], (4, LANES))

        @pl.when(k < NEWTON - 1)
        def _():
            for pair in ((2, 3), (0, 1)):
                new = []
                for s in pair:
                    new.append(newton(
                        [sb[k, s, SIDE * f:SIDE * f + SIDE, :] for f in range(3)], [acc[q, border[s], :] for q in range(7)],
                        fcb[s], mobb[s], dopb[s], eleb[s] == 1,
                    ))
                for s, values in zip(pair, new):
                    for f in range(3):
                        sb[following, s, SIDE * f:SIDE * f + SIDE, :] = values[f]
                start_state(state_copies(following), pair)

        for c in range(CELLS):
            for y in range(CELLS):
                mob[c, 4 * y:4 * y + 4, :] = jnp.broadcast_to(rep[4 * y + c:4 * y + c + 1, :], (4, LANES))

        @pl.when(k == 0)
        def _():
            at = COND_AT
            cx[1, 0:2, :] = keep(has[0], hb[0, 0, at + 2:at + 4, :])
            cx[1, 2:6, :] = sb[0, 0, at:at + 4, :]
            cx[1, 6:8, :] = keep(has[1], hb[0, 1, at:at + 2, :])
            cx[0, 2:6, :] = keep(has[2], hb[0, 2, at:at + 4, :])
            cx[2, 2:6, :] = keep(has[3], hb[0, 3, at:at + 4, :])

        def solve(x, nothing):
            rows = slab(x)
            cell = x // CELLS
            new = newton(
                [st[f, rows, :] for f in range(3)], [acc[q, rows, :] for q in range(7)],
                fc[rows, :], mob[cell], dop[cell], ele[rows, :] == 1,
            )
            for f in range(3):
                st[f, rows, :] = new[f]
            return nothing

        lax.fori_loop(0, SIDE, solve, 0)
        @pl.when(k == 0)
        def _():
            wait_sent(first_copies(), has)

        @pl.when(k > 0)
        def _():
            wait_sent(state_copies(k), has)

        @pl.when(k > 0)
        def _():
            wait_thermal_sent(k)

        return nothing

    lax.fori_loop(0, NEWTON, step, 0)

    wait_thermal(NEWTON)
    temp_ref[0:4, :] = relax(NEWTON)
    wait_thermal_sent(NEWTON)


def emit(st_ref, warm_ref, out_ref, temp_out, temp_ref, sem):
    store = pltpu.make_async_copy(st_ref, out_ref, sem.at[0])
    store.start()
    warm = warm_ref[0:4, :]
    lane4 = lax.broadcasted_iota(jnp.int32, (1, LANES), 1) & 3
    zc = LANES // 4
    cells = jnp.concatenate([jnp.where(lane4 == y, warm, 0.0) for y in range(CELLS)], 0)
    narrow = (lax.broadcasted_iota(jnp.int32, (LANES, zc), 0) // 4 == lax.broadcasted_iota(jnp.int32, (LANES, zc), 1)).astype(F32)
    cells = jnp.dot(cells, narrow, precision=lax.Precision.HIGHEST, preferred_element_type=F32)
    for c in range(CELLS):
        for y in range(CELLS):
            temp_ref[c, y:y + 1, :] = cells[4 * y + c:4 * y + c + 1, :]
    last = pltpu.make_async_copy(temp_ref, temp_out, sem.at[1])
    last.start()
    store.wait()
    last.wait()


def solution(mesh):
    nx, ny = mesh.shape["gx"], mesh.shape["gy"]

    def per_device(sol, ins, ele, imp, con, war):
        vm = pltpu.VMEM
        dma = pltpu.SemaphoreType.DMA
        tile = (SIDE, LANES)
        call = pl.pallas_call(
            functools.partial(body, nx, ny),
            out_shape=(
                pltpu.VMEM((3, NODES, LANES), F32),
                pltpu.VMEM((8, LANES), F32),
            ),
            in_specs=[pl.BlockSpec(memory_space=pl.ANY)] * 6,
            out_specs=(pl.BlockSpec(memory_space=pltpu.VMEM), pl.BlockSpec(memory_space=pltpu.VMEM)),
            scratch_shapes=[
                vm((NODES, LANES), F32),
                vm((NODES, LANES), jnp.int32),
                vm((NODES, LANES), jnp.int32),
                vm((CELLS, CELLS, LANES // 4), jnp.int32),
                vm((CELLS, CELLS, LANES // 4), jnp.int32),
                vm((CELLS, CELLS, LANES // 4), F32),
                vm((3, NODES, LANES), F32),
                vm((NODES, LANES), F32),
                vm((7, NODES, LANES), F32),
                vm((64, LANES), F32),
                vm((64, LANES), F32),
                vm((8, LANES), F32),
                vm((CELLS,) + tile, F32),
                vm((CELLS,) + tile, F32),
                vm((4,) + tile, F32),
                vm((4,) + tile, F32),
                vm((4,) + tile, F32),
                vm((4,) + tile, jnp.int32),
                vm((48, LANES), F32),
                vm((48, LANES // 4), F32),
                vm((4,) + tile, F32),
                vm((NEWTON, 4, FIRST_ROWS, LANES), F32),
                vm((NEWTON, 4, FIRST_ROWS, LANES), F32),
                vm((NEWTON + 1, 8, LANES), F32),
                vm((NEWTON + 1, 4, 2, LANES), F32),
                vm((NEWTON + 1, 4, 8, LANES), F32),
                vm((NEWTON + 1, 4, 2, LANES), F32),
                vm((3, SIDE, LANES), F32),
                vm((3, 8, LANES), F32),
                vm((3, 8, LANES), F32),
                vm((3, 8, LANES), F32),
                vm((8, LANES), F32),
                dma((6,)),
                dma((NEWTON, 4)),
                dma((NEWTON, 4)),
                dma((NEWTON + 1, 4)),
                dma((NEWTON + 1, 4)),
                dma((NEWTON + 1, 4)),
                dma((NEWTON + 1, 4)),
            ],
            compiler_params=pltpu.CompilerParams(collective_id=0, has_side_effects=True),
        )
        state, warm = call(
            sol.reshape(3, NODES, LANES), ins.reshape(NODES, LANES), ele.reshape(NODES, LANES), imp, con, war
        )
        state = pltpu.with_memory_space_constraint(state, pltpu.VMEM)
        warm = pltpu.with_memory_space_constraint(warm, pltpu.VMEM)
        state, warm = pl.pallas_call(
            emit,
            out_shape=(
                jax.ShapeDtypeStruct((3, NODES, LANES), F32),
                jax.ShapeDtypeStruct((CELLS, CELLS, LANES // 4), F32),
            ),
            in_specs=[pl.BlockSpec(memory_space=pltpu.VMEM), pl.BlockSpec(memory_space=pltpu.VMEM)],
            out_specs=(pl.BlockSpec(memory_space=pl.ANY), pl.BlockSpec(memory_space=pl.ANY)),
            scratch_shapes=[vm((CELLS, CELLS, LANES // 4), F32), dma((2,))],
        )(state, warm)
        return state.reshape(3, SIDE, SIDE, LANES), warm

    spec = P("gx", "gy", None)
    return jax.shard_map(
        per_device,
        mesh=mesh,
        in_specs=(P(None, "gx", "gy", None),) + (spec,) * 5,
        out_specs=(P(None, "gx", "gy", None), spec),
        check_vma=False,
    )
```
